32 devices in a mesh: groups: 2 (over y), blk: 16 (over z, x, core).
Axes of the slice: x: 2, y: 2, z: 4, core: 2. Of those that a mesh axis runs over, the one named last changes fastest.
Arguments:
- query_hidden: bfloat16 [512, 32, 768], P(('groups', 'blk')), parts along dimension 0, may hold values from -6 to 6
- passage_hidden: bfloat16 [256, 180, 768], P(('groups', 'blk')), parts along dimension 0, may hold values from -6 to 6
- projection: bfloat16 [768, 128], replicated, may hold values from -0.21875 to 0.21875
- teacher_rows: float32 [512, 32], P(('groups', 'blk')), parts along dimension 0, may hold values from -12 to 12
- teacher_pos: int32 [512], P(('groups', 'blk')), parts along dimension 0, may hold values from 0 to 255, each once
- neg_count: int32 [512], P(('groups', 'blk')), parts along dimension 0, may hold values from 8 to 32
- pass_len: int32 [256], P(('groups', 'blk')), parts along dimension 0, may hold values from 19 to 180
Outputs:
- loss: float32 [512], P(('groups', 'blk')), parts along dimension 0
- grad_w: float32 [1536, 128], P(('groups', 'blk')), parts along dimension 0
The draws below stay inside these ranges and needn't reach their ends.
There are 2 independent parts, one for each index of `groups`. The reference program is written for one: setup_inputs(seed, part) draws one part's arguments, and reference() takes and returns one part's arrays. A program takes and returns all parts, laid end to end along the dimension named above; an argument that names none is the same for every part. Nothing has to cross between parts.
Inputs may be any that keep to these rules, and one draw needn't show every extreme that they name: A permutation: the teacher scores of query q are stored as row teacher_pos[q] of teacher_rows.
All inputs are finite; a program needn't handle non-finite values.
Results may differ from the reference program's by a relative error of at most 0.0073.
Values may be sent and summed in bfloat16 or wider, within the bound.
A program may use at most 128 MiB of HBM per device.

```python
import jax
import jax.numpy as jnp
from jax import lax

H = 768
DIM = 128
QT = 32
PT = 180
CYCLE = 4
Q_DEV = 16
P_DEV = 8
CAND = 32
NQ = 256
NP = 128
N_BLK = 16


def draw_neg_count(key, part):
    counts = jax.random.randint(key, (NQ,), P_DEV, CAND + 1, dtype=jnp.int32)
    return counts.at[0].set(CAND).at[1].set(P_DEV)


def draw_pass_len(key, part):
    lowest = PT // 10 + 1
    lengths = jax.random.randint(key, (NP,), lowest, PT + 1, dtype=jnp.int32)
    return lengths.at[0].set(PT).at[1].set(lowest)


def raised(entries, key, source, target, shards_of, factor):
    def block_of(axis_at):
        return (jnp.arange(entries.shape[axis_at]) // (entries.shape[axis_at] // shards_of)).reshape((-1,) + (1,) * (entries.ndim - 1 - axis_at))

    first = jax.random.permutation(key, shards_of)[block_of(target)]
    other_side = (block_of(target) + shards_of // 2) % shards_of
    return jnp.where((block_of(source) == first) | (block_of(source) == other_side), factor * entries, entries)


def levels(rng, extent, cuts, least, largest):
    factor_of, own = 1.0, jax.random.fold_in(rng, 6)
    for dim, parts in cuts:
        draws = jnp.exp(jax.random.uniform(jax.random.fold_in(own, dim), (parts,), jnp.float32, least / len(cuts), largest / len(cuts)))
        factor_of = factor_of * jnp.repeat(draws, extent[dim] // parts).reshape([-1 if axis == dim else 1 for axis in range(len(extent))])
    return factor_of


def bell_draw(rng, dims, deviation, reach, shards=(), kind=jnp.bfloat16):
    level = levels(rng, dims, shards, -0.22, 0.18) if shards else 1.0
    values = jax.random.normal(rng, dims, jnp.float32) * deviation * level
    return jnp.minimum(jnp.maximum(values, -reach), reach).astype(kind)


def noise_with(key, shape, spread, reach, split, heavy, held_as=jnp.bfloat16):
    drawn = spread * jax.random.normal(key, shape, jnp.float32)
    if split:
        drawn = drawn * levels(key, shape, split, -0.22, 0.18)
    return jnp.clip(raised(drawn, jax.random.fold_in(key, 3), *heavy), -reach, reach).astype(held_as)


def setup_inputs(seed: int = 0, part: int = 0) -> dict:
    key_list = jax.random.split(jax.random.key(seed), 8)
    own_keys = jax.random.split(jax.random.fold_in(key_list[7], part), 8)
    return {
        "query_hidden": noise_with(own_keys[0], (NQ, QT, H), 1.0, 6.0, ((0, 16),), (0, 2, 16, 2.0)),
        "passage_hidden": noise_with(own_keys[1], (NP, PT, H), 1.0, 6.0, ((0, 16),), (0, 2, 16, 2.0)),
        "projection": bell_draw(key_list[2], (H, DIM), H ** -0.5, 0.21875),
        "teacher_rows": bell_draw(own_keys[3], (NQ, CAND), 3.0, 12.0, ((0, 16),), jnp.float32),
        "teacher_pos": jax.random.permutation(own_keys[4], NQ).astype(jnp.int32),
        "neg_count": draw_neg_count(jax.random.fold_in(jax.random.fold_in(key_list[7], part), 71), part),
        "pass_len": draw_pass_len(jax.random.fold_in(jax.random.fold_in(key_list[7], part), 71), part),
    }


smoothing_heat_factor = 0.05
epsilon = 1e-06

def normalize(raw):
    length = jnp.sqrt(lax.optimization_barrier(jnp.sum(raw * raw, axis=1, keepdims=True)) + epsilon)
    return (raw / length, length)

def token_terms(query_flat, passage_flat, lengths):
    count = lengths.shape[0]
    token_affinity_table = lax.dot_general(query_flat, passage_flat, (((1,), (1,)), ((), ())), preferred_element_type=jnp.float32)
    token_affinity_table = token_affinity_table.reshape(query_flat.shape[0], count, -1)
    pairwise_dot_entries = jnp.arange(token_affinity_table.shape[2], dtype=jnp.int32)[None, :] < lengths[:, None]
    natural_power_entries = jnp.where(pairwise_dot_entries[None], jnp.exp(token_affinity_table / smoothing_heat_factor), 0.0)
    return (natural_power_entries, lax.optimization_barrier(jnp.sum(natural_power_entries, axis=2)))

def soft_scores(query_flat, passage_flat, lengths, query_matrix):
    natural_power_entries, power_totals_row = token_terms(query_flat, passage_flat, lengths)
    smooth_peak_values = smoothing_heat_factor * jnp.log(power_totals_row)
    return lax.optimization_barrier(jnp.sum(smooth_peak_values.reshape(query_matrix, -1, lengths.shape[0]), axis=1))

def score_grads(query_flat, passage_flat, lengths, score_grad):
    natural_power_entries, power_totals_row = token_terms(query_flat, passage_flat, lengths)
    rows = query_flat.shape[0]
    query_matrix, count = score_grad.shape
    scale = (score_grad[:, None, :] / power_totals_row.reshape(query_matrix, -1, count)).reshape(rows, count)
    weights = (natural_power_entries * scale[:, :, None]).reshape(rows, -1).astype(jnp.bfloat16)
    query_grad = jnp.dot(weights, passage_flat, preferred_element_type=jnp.float32)
    passage_grad = lax.dot_general(weights, query_flat, (((0,), (0,)), ((), ())), preferred_element_type=jnp.float32)
    return (query_grad, passage_grad)

def kl_terms(student, teacher, counts):
    valid = jnp.arange(student.shape[1], dtype=jnp.int32)[None, :] < counts[:, None]
    student_exp = jnp.where(valid, jnp.exp(student), 0.0)
    student_total = lax.optimization_barrier(jnp.sum(student_exp, axis=1, keepdims=True))
    teacher_exp = jnp.where(valid, jnp.exp(teacher), 0.0)
    teacher_total = lax.optimization_barrier(jnp.sum(teacher_exp, axis=1, keepdims=True))
    student_prob = student_exp / student_total
    teacher_prob = teacher_exp / teacher_total
    gap = teacher - jnp.log(teacher_total) - (student - jnp.log(student_total))
    loss = lax.optimization_barrier(jnp.sum(jnp.where(valid, teacher_prob * gap, 0.0), axis=1))
    return (loss, student_prob - teacher_prob)

def raw_grad(unit, length, grad):
    return ((grad - unit * lax.optimization_barrier(jnp.sum(unit * grad, axis=1, keepdims=True))) / length).astype(jnp.bfloat16)

def block_scores(items):
    return soft_scores(items[0], items[1], items[2], Q_DEV)

def block_grads(items):
    return score_grads(items[0], items[1], items[2], items[3])

def reference(query_hidden, passage_hidden, projection, teacher_rows, teacher_pos, neg_count, pass_len):
    query_flat = query_hidden.reshape(NQ * QT, H)
    passage_flat = passage_hidden.reshape(NP * PT, H)
    query_unit, query_length = normalize(jnp.dot(query_flat, projection, preferred_element_type=jnp.float32))
    passage_unit, passage_length = normalize(jnp.dot(passage_flat, projection, preferred_element_type=jnp.float32))
    query_blocks = query_unit.astype(jnp.bfloat16).reshape(N_BLK, Q_DEV * QT, DIM)
    passage_blocks = passage_unit.astype(jnp.bfloat16).reshape(N_BLK, P_DEV * PT, DIM)
    length_blocks = pass_len.reshape(N_BLK, P_DEV)
    teacher = jnp.take(teacher_rows, teacher_pos, axis=0)
    score_parts = []
    for offset in range(CYCLE):
        moved = jnp.roll(passage_blocks, -offset, axis=0)
        moved_len = jnp.roll(length_blocks, -offset, axis=0)
        score_parts.append(lax.map(block_scores, (query_blocks, moved, moved_len)))
    student = jnp.concatenate(score_parts, axis=2).reshape(NQ, CAND)
    loss, score_grad = kl_terms(student, teacher, neg_count)
    grad_blocks = score_grad.reshape(N_BLK, Q_DEV, CAND)
    query_total = jnp.zeros((N_BLK, Q_DEV * QT, DIM), jnp.float32)
    passage_total = jnp.zeros((N_BLK, P_DEV * PT, DIM), jnp.float32)
    for offset in range(CYCLE):
        moved = jnp.roll(passage_blocks, -offset, axis=0)
        moved_len = jnp.roll(length_blocks, -offset, axis=0)
        portion_derivative = grad_blocks[:, :, offset * P_DEV:(offset + 1) * P_DEV]
        query_part, passage_part = lax.map(block_grads, (query_blocks, moved, moved_len, portion_derivative))
        query_total = query_total + query_part
        passage_total = passage_total + jnp.roll(passage_part, offset, axis=0)
    query_raw = raw_grad(query_unit, query_length, query_total.reshape(NQ * QT, DIM))
    document_unprojected = raw_grad(passage_unit, passage_length, passage_total.reshape(NP * PT, DIM))
    contract = (((0,), (0,)), ((), ()))
    grad_w = lax.dot_general(query_flat, query_raw, contract, preferred_element_type=jnp.float32)
    grad_w = grad_w + lax.dot_general(passage_flat, document_unprojected, contract, preferred_element_type=jnp.float32)
    return (loss, grad_w)
```

```python
import functools
import math

import jax
import jax.numpy as jnp
from jax import lax
from jax.experimental import pallas as pl
from jax.experimental.pallas import tpu as pltpu
from jax.sharding import PartitionSpec as P

CYCLE = 4
HEAT = 0.05
EPSILON = 1e-06
LANES = 128
META = 8
NN = (((1,), (0,)), ((), ()))
NT = (((1,), (1,)), ((), ()))
TN = (((0,), (0,)), ((), ()))
OWN, TWO, DIRECT, FORWARD = range(4)


def dot16(a, b, dims):
    return lax.dot_general(a, b, dims, preferred_element_type=jnp.float32)


def dot32(a, b, dims):
    return lax.dot_general(
        a, b, dims, precision=lax.Precision.HIGHEST, preferred_element_type=jnp.float32
    )


def halves(x):
    high = x.astype(jnp.bfloat16)
    low = (x - high.astype(jnp.float32)).astype(jnp.bfloat16)
    return jnp.concatenate([high, low], axis=0)


def kernel(
    n, queries, q_tokens, passages, p_tokens,
    qh_hbm, ph_hbm, proj_hbm, rows_hbm, pos_hbm, cnt_hbm, len_hbm,
    loss_ref, grad_ref,
    qh, ph, proj, rows_v, pos_v, cnt_v, len_s, in_sem,
    teach, qv, qinv, qt, pv, pinv, pu, put, exps, den, scales, vs, place, pg, rg, pterm, gown,
    z_send, z_recv, l_send, l_recv, f_send, f_recv, t_send, t_recv, d_send, d_recv, part, part_recv,
    teach_ss, teach_rs, q_ss, q_rs, z_ss, z_rs, l_ss, l_rs, g_ss, g_rs, part_ss, part_rs,
):
    me = lax.axis_index("blk")
    core = lax.rem(me, 2)
    sib = me + 1 - 2 * core
    f32, bf16 = jnp.float32, jnp.bfloat16
    q_rows = queries * q_tokens
    p_rows = p_tokens * passages
    padded = pu.shape[1]
    cand = CYCLE * passages

    def peer(shift):
        return lax.rem(me + shift + n, n)

    def remote(src, dst, ss, rs, target):
        return pltpu.make_async_remote_copy(
            src_ref=src, dst_ref=dst, send_sem=ss, recv_sem=rs,
            device_id={"blk": target}, device_id_type=pl.DeviceIdType.MESH,
        )

    def load(src, dst, at):
        return pltpu.make_async_copy(src, dst, in_sem.at[at])

    loads = [
        load(src, dst, at)
        for at, (src, dst) in enumerate(
            [
                (proj_hbm, proj), (qh_hbm, qh), (rows_hbm, rows_v), (pos_hbm, pos_v),
                (cnt_hbm, cnt_v), (len_hbm, len_s), (ph_hbm, ph),
            ]
        )
    ]
    barrier = pltpu.get_barrier_semaphore()

    @pl.loop(1, n)
    def _(k):
        pl.semaphore_signal(
            barrier, inc=1, device_id={"blk": peer(k)}, device_id_type=pl.DeviceIdType.MESH
        )

    for copy in loads:
        copy.start()

    loads[0].wait()
    proj_t = jnp.transpose(proj[...].astype(f32)).astype(bf16)
    loads[1].wait()
    raw = dot16(proj_t, qh[...], NT)
    inv = lax.rsqrt(jnp.sum(raw * raw, axis=0, keepdims=True) + EPSILON)
    qinv[...] = inv
    unit = raw * inv
    qv[...] = unit
    qt[OWN] = unit.astype(bf16)

    for at in range(2, 6):
        loads[at].wait()
    per_row = LANES // cand
    deep = queries // per_row
    pos = pos_v[...]
    local = pos % queries
    meta = [(pos // queries) * META + local % deep, local // deep, cnt_v[...]]
    teach[me] = jnp.concatenate(
        [jnp.concatenate([rows_v[g * deep : (g + 1) * deep] for g in range(per_row)], axis=1)]
        + [jnp.concatenate([x.astype(f32)] * (LANES // queries), axis=1) for x in meta]
        + [jnp.zeros((META - deep - 3, LANES), f32)],
        axis=0,
    )

    pl.semaphore_wait(barrier, n - 1)

    q_two = remote(qt.at[OWN], qt.at[TWO], q_ss.at[0], q_rs.at[0], peer(2))
    q_direct = remote(qt.at[OWN], qt.at[DIRECT], q_ss.at[1], q_rs.at[1], peer(1 + 2 * core))
    q_forward = remote(qt.at[TWO], qt.at[FORWARD], q_ss.at[2], q_rs.at[2], sib)
    q_two.start()
    q_direct.start()

    def teach_send(k):
        return remote(teach.at[me], teach.at[me], teach_ss.at[k], teach_rs.at[k], peer(k))

    def teach_recv(k):
        return remote(teach.at[me], teach.at[peer(-k)], teach_ss.at[k], teach_rs.at[k], peer(k))

    @pl.loop(1, n)
    def _(k):
        teach_send(k).start()

    loads[6].wait()
    step = p_rows // 6
    for c in range(6):
        at = slice(c * step, (c + 1) * step)
        raw_p = dot16(ph[at], proj[...], NN)
        inv_p = lax.rsqrt(jnp.sum(raw_p * raw_p, axis=1, keepdims=True) + EPSILON)
        tokens = slice(c * step // passages, (c + 1) * step // passages)
        pv[tokens] = (raw_p * inv_p).reshape(step // passages, passages, LANES)
        pinv[at] = jnp.broadcast_to(inv_p, raw_p.shape)
    for p in range(passages):
        x = jnp.concatenate(
            [pv[:, p, :], jnp.zeros((padded - p_tokens, LANES), f32)], axis=0
        )
        pu[p] = x.astype(bf16)
        put[p] = jnp.transpose(x).astype(bf16)

    offset_of = {OWN: 0, TWO: 2, DIRECT: 3 - 2 * core, FORWARD: 1 + 2 * core}
    half = CYCLE * queries
    row_q = lax.broadcasted_iota(jnp.int32, (q_rows, LANES), 0) // q_tokens
    lane_q = lax.broadcasted_iota(jnp.int32, (q_rows, LANES), 1) % half
    for slot in range(CYCLE):
        place[slot * q_rows : (slot + 1) * q_rows] = jnp.where(
            lane_q == row_q + offset_of[slot] * queries, 1.0, 0.0
        ).astype(bf16)
    token = lax.broadcasted_iota(jnp.int32, (padded, q_rows), 0)

    def lanes(slot):
        return slice(slot * q_rows, (slot + 1) * q_rows)

    def forward(slot):
        units = qt[slot]
        for p in range(passages):
            sims = dot16(pu[p], units, NN)
            e = jnp.where(
                token < len_s[0, p], jnp.exp2(sims * (math.log2(math.e) / HEAT)), 0.0
            )
            exps[p, :, lanes(slot)] = e.astype(bf16)
            den[p : p + 1, lanes(slot)] = jnp.sum(e, axis=0, keepdims=True)
        peaks = halves(HEAT * jnp.log(den[:, lanes(slot)]))
        placed = dot16(peaks, place[lanes(slot)], NN)
        return placed[:passages] + placed[passages:]

    def products(slot):
        for p in range(passages):
            vs[slot, p] = dot16(put[p], exps[p, :, lanes(slot)], NN)

    student = forward(OWN)
    products(OWN)
    q_two.wait_recv()
    q_forward.start()
    student = student + forward(TWO)
    q_direct.wait_recv()
    student = student + forward(DIRECT)

    for k in range(1, CYCLE):
        teach_recv(k).wait_recv()
    group = lax.broadcasted_iota(jnp.int32, (passages, LANES), 1) % half // queries
    low_half = lax.broadcasted_iota(jnp.int32, (passages, LANES), 1) < half

    def of_blocks(row):
        value = jnp.zeros((passages, LANES), f32)
        for j in range(CYCLE):
            theirs = jnp.broadcast_to(teach[peer(-j), row : row + 1], (passages, LANES))
            value = jnp.where(group == j, theirs, value)
        return value

    counts = of_blocks(deep + 2)
    index = group * passages + lax.broadcasted_iota(jnp.int32, (passages, LANES), 0)
    valid = index.astype(f32) < counts

    q_forward.wait_recv()
    student = student + forward(FORWARD)
    es = jnp.where(valid, jnp.exp(student), 0.0)
    z_own = jnp.broadcast_to(jnp.sum(es, axis=0, keepdims=True), (passages, LANES))
    z_send[...] = z_own

    def z_copy(k):
        at = CYCLE - 1 - k
        return remote(z_send, z_recv.at[at], z_ss.at[at], z_rs.at[at], peer(k))

    shifts = [k for k in range(1 - CYCLE, CYCLE) if k]
    for k in shifts:
        z_copy(k).start()

    for slot in (TWO, DIRECT, FORWARD):
        products(slot)

    @pl.loop(CYCLE, n)
    def _(k):
        teach_recv(k).wait_recv()

    stored = teach[...].reshape(n * META, LANES)
    row_at = of_blocks(deep)[:1]
    part_at = of_blocks(deep + 1)[:1]
    counts_row = counts[:1]
    picks = lax.broadcasted_iota(jnp.int32, (n * META, LANES), 0).astype(f32)
    picked = dot32(stored, jnp.where(picks == row_at, 1.0, 0.0), TN)
    teacher = jnp.zeros((cand, LANES), f32)
    for g in range(per_row):
        teacher = teacher + jnp.where(part_at == g, picked[g * cand : (g + 1) * cand], 0.0)
    ids = lax.broadcasted_iota(jnp.int32, (cand, LANES), 0).astype(f32)
    teacher_exp = jnp.where(ids < counts_row, jnp.exp(teacher), 0.0)
    teacher_total = jnp.sum(teacher_exp, axis=0, keepdims=True)
    all_prob = teacher_exp / teacher_total
    all_log = teacher - jnp.log(teacher_total)
    prob = jnp.zeros((passages, LANES), f32)
    prob_log = jnp.zeros((passages, LANES), f32)
    for j in range(CYCLE):
        at = slice(j * passages, (j + 1) * passages)
        prob = jnp.where(group == j, all_prob[at], prob)
        prob_log = jnp.where(group == j, all_log[at], prob_log)
    cross = jnp.where(valid, prob * (prob_log - student), 0.0)
    cross = jnp.broadcast_to(jnp.sum(cross, axis=0, keepdims=True), (passages, LANES))
    l_send[...] = cross

    def l_copy(k):
        return remote(l_send, l_recv.at[k], l_ss.at[k], l_rs.at[k], peer(-k))

    total = z_own
    for k in shifts:
        z_copy(k).wait_recv()
    for k in shifts:
        moved = pltpu.roll(z_recv[k + CYCLE - 1], (-k * queries) % LANES, 1)
        shared = (group + k >= 0) & (group + k < CYCLE)
        total = total + jnp.where(shared, moved, 0.0)
    score_grad = jnp.where(valid & low_half, es / total - prob, 0.0)
    spread = dot16(halves(score_grad), place[...], NT)
    scales[...] = (spread[:passages] + spread[passages:]) / den[...]

    def combine(slot):
        out = vs[slot, 0] * scales[0:1, lanes(slot)]
        for p in range(1, passages):
            out = out + vs[slot, p] * scales[p : p + 1, lanes(slot)]
        return out

    g_forward = remote(f_send, f_recv, g_ss.at[0], g_rs.at[0], sib)
    g_direct = remote(d_send, d_recv, g_ss.at[1], g_rs.at[1], peer(2 * core - 3))
    g_two = remote(t_send, t_recv, g_ss.at[2], g_rs.at[2], peer(-2))
    f_send[...] = combine(FORWARD).astype(bf16)
    g_forward.start()
    d_send[...] = combine(DIRECT).astype(bf16)
    g_direct.start()
    two = combine(TWO)
    g_forward.wait_recv()
    t_send[...] = (two + f_recv[...].astype(f32)).astype(bf16)
    g_two.start()
    for k in range(1, CYCLE):
        l_copy(k).start()
    gown[...] = combine(OWN)

    for p in range(passages):
        total_p = None
        for slot in range(CYCLE):
            scaled = (qt[slot].astype(f32) * scales[p : p + 1, lanes(slot)]).astype(bf16)
            term = dot16(exps[p, :, lanes(slot)], scaled, NT)
            total_p = term if total_p is None else total_p + term
        pg[:, p, :] = total_p[:p_tokens]
    for c in range(6):
        at = slice(c * step, (c + 1) * step)
        tokens = slice(c * step // passages, (c + 1) * step // passages)
        v = pv[tokens].reshape(step, LANES)
        g = pg[tokens].reshape(step, LANES)
        raw_g = (g - v * jnp.sum(v * g, axis=1, keepdims=True)) * pinv[at]
        rg[at] = raw_g.astype(bf16)
    pterm[...] = dot16(rg[...], ph[...], TN)

    for k in range(1, CYCLE):
        l_copy(k).wait_recv()
        cross = cross + pltpu.roll(l_recv[k], (-k * queries) % LANES, 1)
    loss = cross + jnp.log(total)
    loss_ref[...] = loss[:1, :queries]

    g_direct.wait_recv()
    v = qv[...]
    g = gown[...] + d_recv[...].astype(f32)
    g_two.wait_recv()
    g = g + t_recv[...].astype(f32)
    raw_g = (g - v * jnp.sum(v * g, axis=0, keepdims=True)) * qinv[...]
    whole = jnp.transpose(pterm[...] + dot16(raw_g.astype(bf16), qh[...], NN))
    chunk = grad_ref.shape[0]
    for k in range(n):
        part[k] = whole[k * chunk : (k + 1) * chunk].astype(bf16)

    def part_copy(k):
        return remote(part.at[peer(k)], part_recv.at[k], part_ss.at[k], part_rs.at[k], peer(k))

    @pl.loop(1, n)
    def _(k):
        part_copy(k).start()

    grad_ref[...] = part[me].astype(f32)

    @pl.loop(1, n)
    def _(k):
        part_copy(k).wait_recv()
        grad_ref[...] += part_recv[k].astype(f32)

    q_two.wait_send()
    q_direct.wait_send()
    q_forward.wait_send()
    for k in shifts:
        z_copy(k).wait_send()
    for k in range(1, CYCLE):
        l_copy(k).wait_send()
    g_forward.wait_send()
    g_direct.wait_send()
    g_two.wait_send()

    @pl.loop(1, n)
    def _(k):
        teach_send(k).wait_send()
        part_copy(k).wait_send()


def per_device(
    n, query_hidden, passage_hidden, projection, teacher_rows, teacher_pos, neg_count, pass_len
):
    queries, q_tokens, width = query_hidden.shape
    passages, p_tokens, _ = passage_hidden.shape
    dim = projection.shape[1]
    q_rows = queries * q_tokens
    p_rows = passages * p_tokens
    padded = -(-p_tokens // 16) * 16
    chunk = width // n
    f32, bf16, i32 = jnp.float32, jnp.bfloat16, jnp.int32
    vmem = pl.BlockSpec(memory_space=pltpu.VMEM)
    hbm = pl.BlockSpec(memory_space=pltpu.HBM)
    dma = pltpu.SemaphoreType.DMA
    loss, grad_w = pl.pallas_call(
        functools.partial(kernel, n, queries, q_tokens, passages, p_tokens),
        out_shape=(
            jax.ShapeDtypeStruct((1, queries), f32),
            jax.ShapeDtypeStruct((chunk, dim), f32),
        ),
        in_specs=[hbm] * 7,
        out_specs=(vmem, vmem),
        scratch_shapes=[
            pltpu.VMEM((q_rows, width), bf16),
            pltpu.VMEM((p_rows, width), bf16),
            pltpu.VMEM((width, dim), bf16),
            pltpu.VMEM((queries, CYCLE * passages), f32),
            pltpu.VMEM((1, queries), i32),
            pltpu.VMEM((1, queries), i32),
            pltpu.SMEM((1, passages), i32),
            dma((7,)),
            pltpu.VMEM((n, META, LANES), f32),
            pltpu.VMEM((dim, q_rows), f32),
            pltpu.VMEM((1, q_rows), f32),
            pltpu.VMEM((CYCLE, dim, q_rows), bf16),
            pltpu.VMEM((p_tokens, passages, dim), f32),
            pltpu.VMEM((p_rows, dim), f32),
            pltpu.VMEM((passages, padded, dim), bf16),
            pltpu.VMEM((passages, dim, padded), bf16),
            pltpu.VMEM((passages, padded, CYCLE * q_rows), bf16),
            pltpu.VMEM((passages, CYCLE * q_rows), f32),
            pltpu.VMEM((passages, CYCLE * q_rows), f32),
            pltpu.VMEM((CYCLE, passages, dim, q_rows), f32),
            pltpu.VMEM((CYCLE * q_rows, LANES), bf16),
            pltpu.VMEM((p_tokens, passages, dim), f32),
            pltpu.VMEM((p_rows, dim), bf16),
            pltpu.VMEM((dim, width), f32),
            pltpu.VMEM((dim, q_rows), f32),
            pltpu.VMEM((passages, LANES), f32),
            pltpu.VMEM((2 * CYCLE - 1, passages, LANES), f32),
            pltpu.VMEM((passages, LANES), f32),
            pltpu.VMEM((CYCLE, passages, LANES), f32),
        ]
        + [pltpu.VMEM((dim, q_rows), bf16)] * 6
        + [
            pltpu.VMEM((n, chunk, dim), bf16),
            pltpu.VMEM((n, chunk, dim), bf16),
            dma((n,)), dma((n,)),
            dma((3,)), dma((3,)),
            dma((2 * CYCLE - 1,)), dma((2 * CYCLE - 1,)),
            dma((CYCLE,)), dma((CYCLE,)),
            dma((3,)), dma((3,)),
            dma((n,)), dma((n,)),
        ],
        compiler_params=pltpu.CompilerParams(
            collective_id=0, has_side_effects=True, vmem_limit_bytes=64 * 1024 * 1024
        ),
    )(
        query_hidden.reshape(q_rows, width),
        jnp.transpose(passage_hidden, (1, 0, 2)).reshape(p_rows, width),
        projection,
        teacher_rows,
        teacher_pos.reshape(1, queries),
        neg_count.reshape(1, queries),
        pass_len.reshape(1, passages),
    )
    return (loss.reshape(queries), grad_w)


def solution(mesh):
    return jax.shard_map(
        functools.partial(per_device, mesh.shape["blk"]),
        mesh=mesh,
        in_specs=(
            P(("groups", "blk"), None, None),
            P(("groups", "blk"), None, None),
            P(),
            P(("groups", "blk"), None),
            P(("groups", "blk")),
            P(("groups", "blk")),
            P(("groups", "blk")),
        ),
        out_specs=(P(("groups", "blk")), P(("groups", "blk"), None)),
        check_vma=False,
    )
```

```python
import functools
import math

import jax
import jax.numpy as jnp
from jax import lax
from jax.experimental import pallas as pl
from jax.experimental.pallas import tpu as pltpu
from jax.sharding import PartitionSpec as P

CYCLE = 4
HEAT = 0.05
EPSILON = 1e-06
LANES = 128
META = 8
PARTS = 2
NN = (((1,), (0,)), ((), ()))
NT = (((1,), (1,)), ((), ()))
TN = (((0,), (0,)), ((), ()))
OWN, TWO, DIRECT, FORWARD = range(4)


def dot16(a, b, dims):
    return lax.dot_general(a, b, dims, preferred_element_type=jnp.float32)


def dot32(a, b, dims):
    return lax.dot_general(
        a, b, dims, precision=lax.Precision.HIGHEST, preferred_element_type=jnp.float32
    )


def halves(x):
    high = x.astype(jnp.bfloat16)
    low = (x - high.astype(jnp.float32)).astype(jnp.bfloat16)
    return jnp.concatenate([high, low], axis=0)


def kernel(
    n, queries, q_tokens, passages, p_tokens,
    qh_hbm, ph_hbm, proj_hbm, rows_hbm, pos_hbm, cnt_hbm, len_hbm,
    loss_ref, grad_ref,
    qh, ph, proj, rows_v, pos_v, cnt_v, len_s, in_sem,
    teach, meta, qv, qinv, qt, pv, pinv, pu, put, exps, den, scales, vs, place, pg, rg, pterm, gown,
    z_send, z_recv, l_send, l_recv, f_send, f_recv, t_send, t_recv, d_send, d_recv, part, part_recv,
    teach_ss, teach_rs, meta_ss, meta_rs, q_ss, q_rs, z_ss, z_rs, l_ss, l_rs, g_ss, g_rs, part_ss, part_rs,
):
    me = lax.axis_index("blk")
    core = lax.rem(me, 2)
    sib = me + 1 - 2 * core
    f32, bf16 = jnp.float32, jnp.bfloat16
    q_rows = queries * q_tokens
    p_rows = p_tokens * passages
    padded = pu.shape[1]
    cand = CYCLE * passages

    def peer(shift):
        return lax.rem(me + shift + n, n)

    def remote(src, dst, ss, rs, target):
        return pltpu.make_async_remote_copy(
            src_ref=src, dst_ref=dst, send_sem=ss, recv_sem=rs,
            device_id={"blk": target}, device_id_type=pl.DeviceIdType.MESH,
        )

    def load(src, dst, at):
        return pltpu.make_async_copy(src, dst, in_sem.at[at])

    width_q = q_rows // PARTS

    def piece(h):
        return slice(h * width_q, (h + 1) * width_q)

    load_proj = load(proj_hbm, proj, 0)
    load_q = [load(qh_hbm.at[piece(h)], qh.at[piece(h)], 1 + h) for h in range(PARTS)]
    load_p = load(ph_hbm, ph, 1 + PARTS)
    small = [(rows_hbm, rows_v), (pos_hbm, pos_v), (cnt_hbm, cnt_v), (len_hbm, len_s)]
    load_small = [load(src, dst, 2 + PARTS + at) for at, (src, dst) in enumerate(small)]
    load_proj.start()
    for copy in load_q:
        copy.start()
    barrier = pltpu.get_barrier_semaphore()

    @pl.loop(1, n)
    def _(k):
        pl.semaphore_signal(
            barrier, inc=1, device_id={"blk": peer(k)}, device_id_type=pl.DeviceIdType.MESH
        )

    for copy in load_small:
        copy.start()

    load_proj.wait()
    proj_t = jnp.transpose(proj[...].astype(f32)).astype(bf16)

    def query_units(h):
        load_q[h].wait()
        raw = dot16(proj_t, qh[piece(h)], NT)
        inv = lax.rsqrt(jnp.sum(raw * raw, axis=0, keepdims=True) + EPSILON)
        qinv[:, piece(h)] = inv
        unit = raw * inv
        qv[:, piece(h)] = unit
        qt[OWN, h] = unit.astype(bf16)

    def q_two(h):
        return remote(qt.at[OWN, h], qt.at[TWO, h], q_ss.at[0, h], q_rs.at[0, h], peer(2))

    def q_direct(h):
        return remote(
            qt.at[OWN, h], qt.at[DIRECT, h], q_ss.at[1, h], q_rs.at[1, h], peer(1 + 2 * core)
        )

    def q_forward(h):
        return remote(qt.at[TWO, h], qt.at[FORWARD, h], q_ss.at[2, h], q_rs.at[2, h], sib)

    query_units(0)
    pl.semaphore_wait(barrier, n - 1)
    q_two(0).start()
    q_direct(0).start()
    for h in range(1, PARTS):
        query_units(h)
        q_two(h).start()
        q_direct(h).start()
    load_p.start()

    for copy in load_small:
        copy.wait()
    per_row = LANES // cand
    deep = queries // per_row
    pos = pos_v[...]
    local = pos % queries
    device = pos // queries
    row = (device % 2) * (n // 2 * deep) + (device // 2) * deep + local % deep
    meta[0] = jnp.concatenate(
        [
            jnp.concatenate([x.astype(f32)] * (LANES // queries), axis=1)
            for x in (row, local // deep, cnt_v[...])
        ]
        + [jnp.zeros((META - 3, LANES), f32)],
        axis=0,
    )
    chip = me // 2
    teach[core, chip] = jnp.concatenate(
        [rows_v[g * deep : (g + 1) * deep] for g in range(per_row)], axis=1
    )

    def meta_copy(k):
        return remote(meta.at[0], meta.at[k], meta_ss.at[k], meta_rs.at[k], peer(k))

    for k in range(1, CYCLE):
        meta_copy(k).start()

    def teach_send(k):
        return remote(
            teach.at[core, chip], teach.at[core, chip], teach_ss.at[k], teach_rs.at[k], peer(2 * k)
        )

    def teach_recv(k):
        return remote(
            teach.at[core, chip], teach.at[core, lax.rem(chip - k + n // 2, n // 2)],
            teach_ss.at[k], teach_rs.at[k], peer(2 * k),
        )

    teach_across = remote(teach.at[core], teach.at[core], teach_ss.at[0], teach_rs.at[0], sib)
    teach_from = remote(teach.at[core], teach.at[1 - core], teach_ss.at[0], teach_rs.at[0], sib)

    load_p.wait()
    step = p_rows // 6
    for c in range(6):
        at = slice(c * step, (c + 1) * step)
        raw_p = dot16(ph[at], proj[...], NN)
        inv_p = lax.rsqrt(jnp.sum(raw_p * raw_p, axis=1, keepdims=True) + EPSILON)
        tokens = slice(c * step // passages, (c + 1) * step // passages)
        pv[tokens] = (raw_p * inv_p).reshape(step // passages, passages, LANES)
        pinv[at] = jnp.broadcast_to(inv_p, raw_p.shape)
    for p in range(passages):
        x = jnp.concatenate(
            [pv[:, p, :], jnp.zeros((padded - p_tokens, LANES), f32)], axis=0
        )
        pu[p] = x.astype(bf16)
        put[p] = jnp.transpose(x).astype(bf16)

    offset_of = {OWN: 0, TWO: 2, DIRECT: 3 - 2 * core, FORWARD: 1 + 2 * core}
    half = CYCLE * queries
    row_q = lax.broadcasted_iota(jnp.int32, (q_rows, LANES), 0) // q_tokens
    lane_q = lax.broadcasted_iota(jnp.int32, (q_rows, LANES), 1) % half
    for slot in range(CYCLE):
        place[slot * q_rows : (slot + 1) * q_rows] = jnp.where(
            lane_q == row_q + offset_of[slot] * queries, 1.0, 0.0
        ).astype(bf16)
    token = lax.broadcasted_iota(jnp.int32, (padded, width_q), 0)

    def lanes(slot):
        return slice(slot * q_rows, (slot + 1) * q_rows)

    def part_lanes(slot, h):
        return slice(slot * q_rows + h * width_q, slot * q_rows + (h + 1) * width_q)

    def forward(slot, h):
        units = qt[slot, h]
        at = part_lanes(slot, h)
        for p in range(passages):
            sims = dot16(pu[p], units, NN)
            e = jnp.where(
                token < len_s[0, p], jnp.exp2(sims * (math.log2(math.e) / HEAT)), 0.0
            )
            exps[p, :, at] = e.astype(bf16)
            den[p : p + 1, at] = jnp.sum(e, axis=0, keepdims=True)
        peaks = halves(HEAT * jnp.log(den[:, at]))
        placed = dot16(peaks, place[at], NN)
        return placed[:passages] + placed[passages:]

    def products(slot):
        for p in range(passages):
            vs[slot, p] = dot16(put[p], exps[p, :, lanes(slot)], NN)

    student = forward(OWN, 0) + forward(OWN, 1)
    products(OWN)
    q_two(0).wait_recv()
    q_forward(0).start()
    student = student + forward(TWO, 0)
    q_direct(0).wait_recv()
    student = student + forward(DIRECT, 0)
    q_two(1).wait_recv()
    q_forward(1).start()

    @pl.loop(1, n // 2)
    def _(k):
        teach_send(k).start()

    q_forward(0).wait_recv()
    student = student + forward(FORWARD, 0) + forward(TWO, 1)
    q_direct(1).wait_recv()
    student = student + forward(DIRECT, 1)

    for k in range(1, CYCLE):
        meta_copy(k).wait_recv()
    group = lax.broadcasted_iota(jnp.int32, (passages, LANES), 1) % half // queries
    low_half = lax.broadcasted_iota(jnp.int32, (passages, LANES), 1) < half

    def of_blocks(row):
        value = jnp.zeros((passages, LANES), f32)
        for j in range(CYCLE):
            theirs = jnp.broadcast_to(meta[j, row : row + 1], (passages, LANES))
            value = jnp.where(group == j, theirs, value)
        return value

    counts = of_blocks(2)
    index = group * passages + lax.broadcasted_iota(jnp.int32, (passages, LANES), 0)
    valid = index.astype(f32) < counts

    q_forward(1).wait_recv()
    student = student + forward(FORWARD, 1)
    es = jnp.where(valid, jnp.exp(student), 0.0)
    z_own = jnp.broadcast_to(jnp.sum(es, axis=0, keepdims=True), (passages, LANES))
    z_send[...] = z_own

    def z_copy(k):
        at = CYCLE - 1 - k
        return remote(z_send, z_recv.at[at], z_ss.at[at], z_rs.at[at], peer(k))

    shifts = [k for k in range(1 - CYCLE, CYCLE) if k]
    for k in shifts:
        z_copy(k).start()

    products(TWO)

    @pl.loop(1, n // 2)
    def _(k):
        teach_recv(k).wait_recv()

    teach_across.start()
    products(DIRECT)
    products(FORWARD)

    teach_from.wait_recv()
    stored = teach[...].reshape(n * deep, LANES)
    row_at = of_blocks(0)[:1]
    part_at = of_blocks(1)[:1]
    counts_row = counts[:1]
    picks = lax.broadcasted_iota(jnp.int32, (n * deep, LANES), 0).astype(f32)
    picked = dot32(stored, jnp.where(picks == row_at, 1.0, 0.0), TN)
    teacher = jnp.zeros((cand, LANES), f32)
    for g in range(per_row):
        teacher = teacher + jnp.where(part_at == g, picked[g * cand : (g + 1) * cand], 0.0)
    ids = lax.broadcasted_iota(jnp.int32, (cand, LANES), 0).astype(f32)
    teacher_exp = jnp.where(ids < counts_row, jnp.exp(teacher), 0.0)
    teacher_total = jnp.sum(teacher_exp, axis=0, keepdims=True)
    all_prob = teacher_exp / teacher_total
    all_log = teacher - jnp.log(teacher_total)
    prob = jnp.zeros((passages, LANES), f32)
    prob_log = jnp.zeros((passages, LANES), f32)
    for j in range(CYCLE):
        at = slice(j * passages, (j + 1) * passages)
        prob = jnp.where(group == j, all_prob[at], prob)
        prob_log = jnp.where(group == j, all_log[at], prob_log)
    cross = jnp.where(valid, prob * (prob_log - student), 0.0)
    cross = jnp.broadcast_to(jnp.sum(cross, axis=0, keepdims=True), (passages, LANES))
    l_send[...] = cross

    def l_copy(k):
        return remote(l_send, l_recv.at[k], l_ss.at[k], l_rs.at[k], peer(-k))

    total = z_own
    for k in shifts:
        z_copy(k).wait_recv()
    for k in shifts:
        moved = pltpu.roll(z_recv[k + CYCLE - 1], (-k * queries) % LANES, 1)
        shared = (group + k >= 0) & (group + k < CYCLE)
        total = total + jnp.where(shared, moved, 0.0)
    score_grad = jnp.where(valid & low_half, es / total - prob, 0.0)
    spread = dot16(halves(score_grad), place[...], NT)
    scales[...] = (spread[:passages] + spread[passages:]) / den[...]

    def combine(slot, h):
        at = part_lanes(slot, h)
        out = vs[slot, 0, :, piece(h)] * scales[0:1, at]
        for p in range(1, passages):
            out = out + vs[slot, p, :, piece(h)] * scales[p : p + 1, at]
        return out

    def g_forward(h):
        return remote(f_send.at[h], f_recv.at[h], g_ss.at[0, h], g_rs.at[0, h], sib)

    def g_direct(h):
        return remote(d_send.at[h], d_recv.at[h], g_ss.at[1, h], g_rs.at[1, h], peer(2 * core - 3))

    def g_two(h):
        return remote(t_send.at[h], t_recv.at[h], g_ss.at[2, h], g_rs.at[2, h], peer(-2))

    for h in range(PARTS):
        f_send[h] = combine(FORWARD, h).astype(bf16)
        g_forward(h).start()
    for h in range(PARTS):
        d_send[h] = combine(DIRECT, h).astype(bf16)
        g_direct(h).start()
    for h in range(PARTS):
        two = combine(TWO, h)
        g_forward(h).wait_recv()
        t_send[h] = (two + f_recv[h].astype(f32)).astype(bf16)
        g_two(h).start()
    for k in range(1, CYCLE):
        l_copy(k).start()
    for h in range(PARTS):
        gown[:, piece(h)] = combine(OWN, h)

    for p in range(passages):
        total_p = None
        for slot in range(CYCLE):
            for h in range(PARTS):
                at = part_lanes(slot, h)
                scaled = (qt[slot, h].astype(f32) * scales[p : p + 1, at]).astype(bf16)
                term = dot16(exps[p, :, at], scaled, NT)
                total_p = term if total_p is None else total_p + term
        pg[:, p, :] = total_p[:p_tokens]
    for c in range(6):
        at = slice(c * step, (c + 1) * step)
        tokens = slice(c * step // passages, (c + 1) * step // passages)
        v = pv[tokens].reshape(step, LANES)
        g = pg[tokens].reshape(step, LANES)
        raw_g = (g - v * jnp.sum(v * g, axis=1, keepdims=True)) * pinv[at]
        rg[at] = raw_g.astype(bf16)
    pterm[...] = dot16(rg[...], ph[...], TN)

    for k in range(1, CYCLE):
        l_copy(k).wait_recv()
        cross = cross + pltpu.roll(l_recv[k], (-k * queries) % LANES, 1)
    loss = cross + jnp.log(total)
    loss_ref[...] = loss[:1, :queries]

    whole = pterm[...]
    for h in range(PARTS):
        g_direct(h).wait_recv()
        g_two(h).wait_recv()
        v = qv[:, piece(h)]
        g = gown[:, piece(h)] + d_recv[h].astype(f32) + t_recv[h].astype(f32)
        raw_g = (g - v * jnp.sum(v * g, axis=0, keepdims=True)) * qinv[:, piece(h)]
        whole = whole + dot16(raw_g.astype(bf16), qh[piece(h)], NN)
    whole = jnp.transpose(whole)
    chunk = grad_ref.shape[0]
    for k in range(n):
        part[k] = whole[k * chunk : (k + 1) * chunk].astype(bf16)

    def part_copy(k):
        return remote(part.at[peer(k)], part_recv.at[k], part_ss.at[k], part_rs.at[k], peer(k))

    @pl.loop(1, n)
    def _(k):
        part_copy(k).start()

    grad_ref[...] = part[me].astype(f32)

    @pl.loop(1, n)
    def _(k):
        part_copy(k).wait_recv()
        grad_ref[...] += part_recv[k].astype(f32)

    for h in range(PARTS):
        q_two(h).wait_send()
        q_direct(h).wait_send()
        q_forward(h).wait_send()
        g_forward(h).wait_send()
        g_direct(h).wait_send()
        g_two(h).wait_send()
    for k in shifts:
        z_copy(k).wait_send()
    for k in range(1, CYCLE):
        meta_copy(k).wait_send()
        l_copy(k).wait_send()
    teach_across.wait_send()

    @pl.loop(1, n // 2)
    def _(k):
        teach_send(k).wait_send()

    @pl.loop(1, n)
    def _(k):
        part_copy(k).wait_send()


def per_device(
    n, query_hidden, passage_hidden, projection, teacher_rows, teacher_pos, neg_count, pass_len
):
    queries, q_tokens, width = query_hidden.shape
    passages, p_tokens, _ = passage_hidden.shape
    dim = projection.shape[1]
    q_rows = queries * q_tokens
    p_rows = passages * p_tokens
    padded = -(-p_tokens // 16) * 16
    chunk = width // n
    f32, bf16, i32 = jnp.float32, jnp.bfloat16, jnp.int32
    vmem = pl.BlockSpec(memory_space=pltpu.VMEM)
    hbm = pl.BlockSpec(memory_space=pltpu.HBM)
    dma = pltpu.SemaphoreType.DMA
    loss, grad_w = pl.pallas_call(
        functools.partial(kernel, n, queries, q_tokens, passages, p_tokens),
        out_shape=(
            jax.ShapeDtypeStruct((1, queries), f32),
            jax.ShapeDtypeStruct((chunk, dim), f32),
        ),
        in_specs=[hbm] * 7,
        out_specs=(vmem, vmem),
        scratch_shapes=[
            pltpu.VMEM((q_rows, width), bf16),
            pltpu.VMEM((p_rows, width), bf16),
            pltpu.VMEM((width, dim), bf16),
            pltpu.VMEM((queries, CYCLE * passages), f32),
            pltpu.VMEM((1, queries), i32),
            pltpu.VMEM((1, queries), i32),
            pltpu.SMEM((1, passages), i32),
            dma((6 + PARTS,)),
            pltpu.VMEM((2, n // 2, queries * CYCLE * passages // LANES, LANES), f32),
            pltpu.VMEM((CYCLE, META, LANES), f32),
            pltpu.VMEM((dim, q_rows), f32),
            pltpu.VMEM((1, q_rows), f32),
            pltpu.VMEM((CYCLE, PARTS, dim, q_rows // PARTS), bf16),
            pltpu.VMEM((p_tokens, passages, dim), f32),
            pltpu.VMEM((p_rows, dim), f32),
            pltpu.VMEM((passages, padded, dim), bf16),
            pltpu.VMEM((passages, dim, padded), bf16),
            pltpu.VMEM((passages, padded, CYCLE * q_rows), bf16),
            pltpu.VMEM((passages, CYCLE * q_rows), f32),
            pltpu.VMEM((passages, CYCLE * q_rows), f32),
            pltpu.VMEM((CYCLE, passages, dim, q_rows), f32),
            pltpu.VMEM((CYCLE * q_rows, LANES), bf16),
            pltpu.VMEM((p_tokens, passages, dim), f32),
            pltpu.VMEM((p_rows, dim), bf16),
            pltpu.VMEM((dim, width), f32),
            pltpu.VMEM((dim, q_rows), f32),
            pltpu.VMEM((passages, LANES), f32),
            pltpu.VMEM((2 * CYCLE - 1, passages, LANES), f32),
            pltpu.VMEM((passages, LANES), f32),
            pltpu.VMEM((CYCLE, passages, LANES), f32),
        ]
        + [pltpu.VMEM((PARTS, dim, q_rows // PARTS), bf16)] * 6
        + [
            pltpu.VMEM((n, chunk, dim), bf16),
            pltpu.VMEM((n, chunk, dim), bf16),
            dma((n // 2,)), dma((n // 2,)),
            dma((CYCLE,)), dma((CYCLE,)),
            dma((3, PARTS)), dma((3, PARTS)),
            dma((2 * CYCLE - 1,)), dma((2 * CYCLE - 1,)),
            dma((CYCLE,)), dma((CYCLE,)),
            dma((3, PARTS)), dma((3, PARTS)),
            dma((n,)), dma((n,)),
        ],
        compiler_params=pltpu.CompilerParams(
            collective_id=0, has_side_effects=True, vmem_limit_bytes=50 * 1024 * 1024
        ),
    )(
        *[
            pltpu.with_memory_space_constraint(x, pltpu.HBM)
            for x in (
                query_hidden.reshape(q_rows, width),
                jnp.transpose(passage_hidden, (1, 0, 2)).reshape(p_rows, width),
                projection,
                teacher_rows,
                teacher_pos.reshape(1, queries),
                neg_count.reshape(1, queries),
                pass_len.reshape(1, passages),
            )
        ]
    )
    return (loss.reshape(queries), grad_w)


def solution(mesh):
    return jax.shard_map(
        functools.partial(per_device, mesh.shape["blk"]),
        mesh=mesh,
        in_specs=(
            P(("groups", "blk"), None, None),
            P(("groups", "blk"), None, None),
            P(),
            P(("groups", "blk"), None),
            P(("groups", "blk")),
            P(("groups", "blk")),
            P(("groups", "blk")),
        ),
        out_specs=(P(("groups", "blk")), P(("groups", "blk"), None)),
        check_vma=False,
    )
```

```python
import functools
import math

import jax
import jax.numpy as jnp
from jax import lax
from jax.experimental import pallas as pl
from jax.experimental.pallas import tpu as pltpu
from jax.sharding import PartitionSpec as P

CYCLE = 4
HEAT = 0.05
EPSILON = 1e-06
LANES = 128
META = 8
PARTS = 2
NN = (((1,), (0,)), ((), ()))
NT = (((1,), (1,)), ((), ()))
TN = (((0,), (0,)), ((), ()))
OWN, TWO, DIRECT, FORWARD = range(4)


def dot16(a, b, dims):
    return lax.dot_general(a, b, dims, preferred_element_type=jnp.float32)


def dot32(a, b, dims):
    return lax.dot_general(
        a, b, dims, precision=lax.Precision.HIGHEST, preferred_element_type=jnp.float32
    )


def halves(x):
    high = x.astype(jnp.bfloat16)
    low = (x - high.astype(jnp.float32)).astype(jnp.bfloat16)
    return jnp.concatenate([high, low], axis=0)


def kernel(
    n, queries, q_tokens, passages, p_tokens,
    qh_hbm, ph_hbm, proj_hbm, rows_hbm, pos_hbm, cnt_hbm, len_hbm,
    loss_ref, grad_ref,
    qh, ph, proj, rows_v, pos_v, cnt_v, len_s, in_sem,
    teach, qv, qinv, qt, pv, pinv, pu, put, exps, den, scales, vs, place, pg, rg, pterm, gown,
    z_send, z_recv, f_send, f_recv, t_send, t_recv, d_send, d_recv, part, part_recv,
    teach_ss, teach_rs, q_ss, q_rs, z_ss, z_rs, g_ss, g_rs, part_ss, part_rs,
):
    me = lax.axis_index("blk")
    core = lax.rem(me, 2)
    sib = me + 1 - 2 * core
    f32, bf16 = jnp.float32, jnp.bfloat16
    q_rows = queries * q_tokens
    p_rows = p_tokens * passages
    padded = pu.shape[1]
    cand = CYCLE * passages

    def peer(shift):
        return lax.rem(me + shift + n, n)

    def remote(src, dst, ss, rs, target):
        return pltpu.make_async_remote_copy(
            src_ref=src, dst_ref=dst, send_sem=ss, recv_sem=rs,
            device_id={"blk": target}, device_id_type=pl.DeviceIdType.MESH,
        )

    def load(src, dst, at):
        return pltpu.make_async_copy(src, dst, in_sem.at[at])

    width_q = q_rows // PARTS

    def piece(h):
        return slice(h * width_q, (h + 1) * width_q)

    load_proj = load(proj_hbm, proj, 0)
    load_q = [load(qh_hbm.at[piece(h)], qh.at[piece(h)], 1 + h) for h in range(PARTS)]
    load_p = load(ph_hbm, ph, 1 + PARTS)
    small = [(rows_hbm, rows_v), (pos_hbm, pos_v), (cnt_hbm, cnt_v), (len_hbm, len_s)]
    load_small = [load(src, dst, 2 + PARTS + at) for at, (src, dst) in enumerate(small)]
    load_proj.start()
    for copy in load_q:
        copy.start()
    barrier = pltpu.get_barrier_semaphore()

    @pl.loop(1, n)
    def _(k):
        pl.semaphore_signal(
            barrier, inc=1, device_id={"blk": peer(k)}, device_id_type=pl.DeviceIdType.MESH
        )

    for copy in load_small:
        copy.start()

    load_proj.wait()
    proj_t = jnp.transpose(proj[...].astype(f32)).astype(bf16)

    def query_units(h):
        load_q[h].wait()
        raw = dot16(proj_t, qh[piece(h)], NT)
        inv = lax.rsqrt(jnp.sum(raw * raw, axis=0, keepdims=True) + EPSILON)
        qinv[:, piece(h)] = inv
        unit = raw * inv
        qv[:, piece(h)] = unit
        qt[OWN, h] = unit.astype(bf16)

    def q_two(h):
        return remote(qt.at[OWN, h], qt.at[TWO, h], q_ss.at[0, h], q_rs.at[0, h], peer(2))

    def q_direct(h):
        return remote(
            qt.at[OWN, h], qt.at[DIRECT, h], q_ss.at[1, h], q_rs.at[1, h], peer(1 + 2 * core)
        )

    def q_forward(h):
        return remote(qt.at[TWO, h], qt.at[FORWARD, h], q_ss.at[2, h], q_rs.at[2, h], sib)

    query_units(0)
    pl.semaphore_wait(barrier, n - 1)
    q_two(0).start()
    q_direct(0).start()
    for h in range(1, PARTS):
        query_units(h)
        q_two(h).start()
        q_direct(h).start()
    load_p.start()

    for copy in load_small:
        copy.wait()
    per_row = LANES // cand
    deep = queries // per_row
    pos = pos_v[...]
    local = pos % queries
    device = pos // queries
    row = ((device % 2) * (n // 2) + device // 2) * META + local % deep
    chip = me // 2
    teach[core, chip] = jnp.concatenate(
        [jnp.concatenate([rows_v[g * deep : (g + 1) * deep] for g in range(per_row)], axis=1)]
        + [
            jnp.concatenate([x.astype(f32)] * (LANES // queries), axis=1)
            for x in (row, local // deep, cnt_v[...])
        ]
        + [jnp.zeros((META - deep - 3, LANES), f32)],
        axis=0,
    )

    def teach_send(k):
        return remote(
            teach.at[core, chip], teach.at[core, chip], teach_ss.at[k], teach_rs.at[k], peer(2 * k)
        )

    def teach_recv(k):
        return remote(
            teach.at[core, chip], teach.at[core, lax.rem(chip - k + n // 2, n // 2)],
            teach_ss.at[k], teach_rs.at[k], peer(2 * k),
        )

    teach_across = remote(teach.at[core], teach.at[core], teach_ss.at[0], teach_rs.at[0], sib)
    teach_from = remote(teach.at[core], teach.at[1 - core], teach_ss.at[0], teach_rs.at[0], sib)

    load_p.wait()
    step = p_rows // 6
    for c in range(6):
        at = slice(c * step, (c + 1) * step)
        raw_p = dot16(ph[at], proj[...], NN)
        inv_p = lax.rsqrt(jnp.sum(raw_p * raw_p, axis=1, keepdims=True) + EPSILON)
        tokens = slice(c * step // passages, (c + 1) * step // passages)
        pv[tokens] = (raw_p * inv_p).reshape(step // passages, passages, LANES)
        pinv[at] = jnp.broadcast_to(inv_p, raw_p.shape)
    for p in range(passages):
        x = jnp.concatenate(
            [pv[:, p, :], jnp.zeros((padded - p_tokens, LANES), f32)], axis=0
        )
        pu[p] = x.astype(bf16)
        put[p] = jnp.transpose(x).astype(bf16)

    offset_of = {OWN: 0, TWO: 2, DIRECT: 3 - 2 * core, FORWARD: 1 + 2 * core}
    half = CYCLE * queries
    row_q = lax.broadcasted_iota(jnp.int32, (q_rows, LANES), 0) // q_tokens
    lane_q = lax.broadcasted_iota(jnp.int32, (q_rows, LANES), 1) % half
    for slot in range(CYCLE):
        place[slot * q_rows : (slot + 1) * q_rows] = jnp.where(
            lane_q == row_q + offset_of[slot] * queries, 1.0, 0.0
        ).astype(bf16)
    token = lax.broadcasted_iota(jnp.int32, (padded, width_q), 0)

    def lanes(slot):
        return slice(slot * q_rows, (slot + 1) * q_rows)

    def part_lanes(slot, h):
        return slice(slot * q_rows + h * width_q, slot * q_rows + (h + 1) * width_q)

    def forward(slot, h):
        units = qt[slot, h]
        at = part_lanes(slot, h)
        for p in range(passages):
            sims = dot16(pu[p], units, NN)
            e = jnp.where(
                token < len_s[0, p], jnp.exp2(sims * (math.log2(math.e) / HEAT)), 0.0
            )
            exps[p, :, at] = e.astype(bf16)
            den[p : p + 1, at] = jnp.sum(e, axis=0, keepdims=True)
        peaks = halves(HEAT * jnp.log(den[:, at]))
        placed = dot16(peaks, place[at], NN)
        return placed[:passages] + placed[passages:]

    def products(slot):
        for p in range(passages):
            vs[slot, p] = dot16(put[p], exps[p, :, lanes(slot)], NN)

    student = forward(OWN, 0) + forward(OWN, 1)
    products(OWN)
    q_two(0).wait_recv()
    q_forward(0).start()
    student = student + forward(TWO, 0)
    q_direct(0).wait_recv()
    student = student + forward(DIRECT, 0)
    q_two(1).wait_recv()
    q_forward(1).start()

    @pl.loop(1, n // 2)
    def _(k):
        teach_send(k).start()

    q_forward(0).wait_recv()
    student = student + forward(FORWARD, 0) + forward(TWO, 1)
    q_direct(1).wait_recv()
    student = student + forward(DIRECT, 1)

    q_forward(1).wait_recv()
    student = student + forward(FORWARD, 1)
    z_send[...] = student

    def z_copy(k):
        at = CYCLE - 1 - k
        return remote(z_send, z_recv.at[at], z_ss.at[at], z_rs.at[at], peer(k))

    shifts = [k for k in range(1 - CYCLE, CYCLE) if k]
    for k in shifts:
        z_copy(k).start()

    products(TWO)

    @pl.loop(1, n // 2)
    def _(k):
        teach_recv(k).wait_recv()

    teach_across.start()
    products(DIRECT)
    products(FORWARD)

    group = lax.broadcasted_iota(jnp.int32, (passages, LANES), 1) % half // queries
    low_half = lax.broadcasted_iota(jnp.int32, (passages, LANES), 1) < half
    passage = lax.broadcasted_iota(jnp.int32, (passages, LANES), 0)

    def of_blocks(row):
        value = jnp.zeros((passages, LANES), f32)
        for j in range(CYCLE):
            at = peer(-j)
            theirs = teach[lax.rem(at, 2), at // 2, deep + row : deep + row + 1]
            value = jnp.where(group == j, jnp.broadcast_to(theirs, (passages, LANES)), value)
        return value

    teach_from.wait_recv()
    stored = teach[...].reshape(n * META, LANES)
    counts = of_blocks(2)
    row_at = of_blocks(0)[:1]
    part_at = of_blocks(1)[:1]
    counts_row = counts[:1]
    picks = lax.broadcasted_iota(jnp.int32, (n * META, LANES), 0).astype(f32)
    picked = dot32(stored, jnp.where(picks == row_at, 1.0, 0.0), TN)
    teacher = jnp.zeros((cand, LANES), f32)
    for g in range(per_row):
        teacher = teacher + jnp.where(part_at == g, picked[g * cand : (g + 1) * cand], 0.0)
    ids = lax.broadcasted_iota(jnp.int32, (cand, LANES), 0).astype(f32)
    teacher_exp = jnp.where(ids < counts_row, jnp.exp(teacher), 0.0)
    teacher_total = jnp.sum(teacher_exp, axis=0, keepdims=True)
    all_prob = teacher_exp / teacher_total
    all_log = teacher - jnp.log(teacher_total)
    prob = jnp.zeros((passages, LANES), f32)
    for j in range(CYCLE):
        prob = jnp.where(group == j, all_prob[j * passages : (j + 1) * passages], prob)

    def valid(k):
        index = ((group + k) * passages + passage).astype(f32)
        return (group + k >= 0) & (group + k < CYCLE) & (index < counts)

    es = jnp.where(valid(0), jnp.exp(student), 0.0)
    masks = {k: valid(k) for k in shifts}
    for k in shifts:
        z_copy(k).wait_recv()
    own_scores = [student]
    all_es = es
    for k in shifts:
        moved = pltpu.roll(z_recv[k + CYCLE - 1], (-k * queries) % LANES, 1)
        all_es = all_es + jnp.where(masks[k], jnp.exp(moved), 0.0)
        if k > 0:
            own_scores.append(moved)
    total = jnp.sum(all_es, axis=0, keepdims=True)
    score_grad = jnp.where(valid(0) & low_half, es / total - prob, 0.0)
    spread = dot16(halves(score_grad), place[...], NT)
    scales[...] = (spread[:passages] + spread[passages:]) / den[...]

    def combine(slot, h):
        at = part_lanes(slot, h)
        out = vs[slot, 0, :, piece(h)] * scales[0:1, at]
        for p in range(1, passages):
            out = out + vs[slot, p, :, piece(h)] * scales[p : p + 1, at]
        return out

    def g_forward(h):
        return remote(f_send.at[h], f_recv.at[h], g_ss.at[0, h], g_rs.at[0, h], sib)

    def g_direct(h):
        return remote(d_send.at[h], d_recv.at[h], g_ss.at[1, h], g_rs.at[1, h], peer(2 * core - 3))

    def g_two(h):
        return remote(t_send.at[h], t_recv.at[h], g_ss.at[2, h], g_rs.at[2, h], peer(-2))

    for h in range(PARTS):
        f_send[h] = combine(FORWARD, h).astype(bf16)
        g_forward(h).start()
    for h in range(PARTS):
        d_send[h] = combine(DIRECT, h).astype(bf16)
        g_direct(h).start()
    for h in range(PARTS):
        two = combine(TWO, h)
        g_forward(h).wait_recv()
        t_send[h] = (two + f_recv[h].astype(f32)).astype(bf16)
        g_two(h).start()
    for h in range(PARTS):
        gown[:, piece(h)] = combine(OWN, h)

    for p in range(passages):
        total_p = None
        for slot in range(CYCLE):
            for h in range(PARTS):
                at = part_lanes(slot, h)
                scaled = (qt[slot, h].astype(f32) * scales[p : p + 1, at]).astype(bf16)
                term = dot16(exps[p, :, at], scaled, NT)
                total_p = term if total_p is None else total_p + term
        pg[:, p, :] = total_p[:p_tokens]
    for c in range(6):
        at = slice(c * step, (c + 1) * step)
        tokens = slice(c * step // passages, (c + 1) * step // passages)
        v = pv[tokens].reshape(step, LANES)
        g = pg[tokens].reshape(step, LANES)
        raw_g = (g - v * jnp.sum(v * g, axis=1, keepdims=True)) * pinv[at]
        rg[at] = raw_g.astype(bf16)
    pterm[...] = dot16(rg[...], ph[...], TN)

    gap = all_log - (jnp.concatenate(own_scores, axis=0) - jnp.log(total))
    gap = jnp.where(ids < counts_row, all_prob * gap, 0.0)
    loss = jnp.sum(gap, axis=0, keepdims=True)
    loss_ref[...] = loss[:, :queries]

    whole = pterm[...]
    for h in range(PARTS):
        g_direct(h).wait_recv()
        g_two(h).wait_recv()
        v = qv[:, piece(h)]
        g = gown[:, piece(h)] + d_recv[h].astype(f32) + t_recv[h].astype(f32)
        raw_g = (g - v * jnp.sum(v * g, axis=0, keepdims=True)) * qinv[:, piece(h)]
        whole = whole + dot16(raw_g.astype(bf16), qh[piece(h)], NN)
    whole = jnp.transpose(whole)
    chunk = grad_ref.shape[0]
    for k in range(n):
        part[k] = whole[k * chunk : (k + 1) * chunk].astype(bf16)

    def part_copy(k):
        return remote(part.at[peer(k)], part_recv.at[k], part_ss.at[k], part_rs.at[k], peer(k))

    @pl.loop(1, n)
    def _(k):
        part_copy(k).start()

    grad_ref[...] = part[me].astype(f32)

    @pl.loop(1, n)
    def _(k):
        part_copy(k).wait_recv()
        grad_ref[...] += part_recv[k].astype(f32)

    for h in range(PARTS):
        q_two(h).wait_send()
        q_direct(h).wait_send()
        q_forward(h).wait_send()
        g_forward(h).wait_send()
        g_direct(h).wait_send()
        g_two(h).wait_send()
    for k in shifts:
        z_copy(k).wait_send()
    teach_across.wait_send()

    @pl.loop(1, n // 2)
    def _(k):
        teach_send(k).wait_send()

    @pl.loop(1, n)
    def _(k):
        part_copy(k).wait_send()


def per_device(
    n, query_hidden, passage_hidden, projection, teacher_rows, teacher_pos, neg_count, pass_len
):
    queries, q_tokens, width = query_hidden.shape
    passages, p_tokens, _ = passage_hidden.shape
    dim = projection.shape[1]
    q_rows = queries * q_tokens
    p_rows = passages * p_tokens
    padded = -(-p_tokens // 16) * 16
    chunk = width // n
    f32, bf16, i32 = jnp.float32, jnp.bfloat16, jnp.int32
    vmem = pl.BlockSpec(memory_space=pltpu.VMEM)
    hbm = pl.BlockSpec(memory_space=pltpu.HBM)
    dma = pltpu.SemaphoreType.DMA
    loss, grad_w = pl.pallas_call(
        functools.partial(kernel, n, queries, q_tokens, passages, p_tokens),
        out_shape=(
            jax.ShapeDtypeStruct((1, queries), f32),
            jax.ShapeDtypeStruct((chunk, dim), f32),
        ),
        in_specs=[hbm] * 7,
        out_specs=(vmem, vmem),
        scratch_shapes=[
            pltpu.VMEM((q_rows, width), bf16),
            pltpu.VMEM((p_rows, width), bf16),
            pltpu.VMEM((width, dim), bf16),
            pltpu.VMEM((queries, CYCLE * passages), f32),
            pltpu.VMEM((1, queries), i32),
            pltpu.VMEM((1, queries), i32),
            pltpu.SMEM((1, passages), i32),
            dma((6 + PARTS,)),
            pltpu.VMEM((2, n // 2, META, LANES), f32),
            pltpu.VMEM((dim, q_rows), f32),
            pltpu.VMEM((1, q_rows), f32),
            pltpu.VMEM((CYCLE, PARTS, dim, q_rows // PARTS), bf16),
            pltpu.VMEM((p_tokens, passages, dim), f32),
            pltpu.VMEM((p_rows, dim), f32),
            pltpu.VMEM((passages, padded, dim), bf16),
            pltpu.VMEM((passages, dim, padded), bf16),
            pltpu.VMEM((passages, padded, CYCLE * q_rows), bf16),
            pltpu.VMEM((passages, CYCLE * q_rows), f32),
            pltpu.VMEM((passages, CYCLE * q_rows), f32),
            pltpu.VMEM((CYCLE, passages, dim, q_rows), f32),
            pltpu.VMEM((CYCLE * q_rows, LANES), bf16),
            pltpu.VMEM((p_tokens, passages, dim), f32),
            pltpu.VMEM((p_rows, dim), bf16),
            pltpu.VMEM((dim, width), f32),
            pltpu.VMEM((dim, q_rows), f32),
            pltpu.VMEM((passages, LANES), f32),
            pltpu.VMEM((2 * CYCLE - 1, passages, LANES), f32),
        ]
        + [pltpu.VMEM((PARTS, dim, q_rows // PARTS), bf16)] * 6
        + [
            pltpu.VMEM((n, chunk, dim), bf16),
            pltpu.VMEM((n, chunk, dim), bf16),
            dma((n // 2,)), dma((n // 2,)),
            dma((3, PARTS)), dma((3, PARTS)),
            dma((2 * CYCLE - 1,)), dma((2 * CYCLE - 1,)),
            dma((3, PARTS)), dma((3, PARTS)),
            dma((n,)), dma((n,)),
        ],
        compiler_params=pltpu.CompilerParams(
            collective_id=0, has_side_effects=True, vmem_limit_bytes=50 * 1024 * 1024
        ),
    )(
        *[
            pltpu.with_memory_space_constraint(x, pltpu.HBM)
            for x in (
                query_hidden.reshape(q_rows, width),
                jnp.transpose(passage_hidden, (1, 0, 2)).reshape(p_rows, width),
                projection,
                teacher_rows,
                teacher_pos.reshape(1, queries),
                neg_count.reshape(1, queries),
                pass_len.reshape(1, passages),
            )
        ]
    )
    return (loss.reshape(queries), grad_w)


def solution(mesh):
    return jax.shard_map(
        functools.partial(per_device, mesh.shape["blk"]),
        mesh=mesh,
        in_specs=(
            P(("groups", "blk"), None, None),
            P(("groups", "blk"), None, None),
            P(),
            P(("groups", "blk"), None),
            P(("groups", "blk")),
            P(("groups", "blk")),
            P(("groups", "blk")),
        ),
        out_specs=(P(("groups", "blk")), P(("groups", "blk"), None)),
        check_vma=False,
    )
```

```python
import functools
import math

import jax
import jax.numpy as jnp
from jax import lax
from jax.experimental import pallas as pl
from jax.experimental.pallas import tpu as pltpu
from jax.sharding import PartitionSpec as P

CYCLE = 4
HEAT = 0.05
EPSILON = 1e-06
LANES = 128
META = 8
PARTS = 2
NN = (((1,), (0,)), ((), ()))
NT = (((1,), (1,)), ((), ()))
TN = (((0,), (0,)), ((), ()))
OWN, TWO, DIRECT, FORWARD = range(4)


def dot16(a, b, dims):
    return lax.dot_general(a, b, dims, preferred_element_type=jnp.float32)


def dot32(a, b, dims):
    return lax.dot_general(
        a, b, dims, precision=lax.Precision.HIGHEST, preferred_element_type=jnp.float32
    )


def halves(x):
    high = x.astype(jnp.bfloat16)
    low = (x - high.astype(jnp.float32)).astype(jnp.bfloat16)
    return jnp.concatenate([high, low], axis=0)


def kernel(
    n, queries, q_tokens, passages, p_tokens,
    qh_hbm, ph_hbm, proj_hbm, rows_hbm, pos_hbm, cnt_hbm, len_hbm,
    loss_ref, grad_ref,
    qh, ph, proj, rows_v, pos_v, cnt_v, len_s, in_sem,
    teach, qv, qinv, qt, pv, pinv, pu, put, exps, den, scales, vs, place, pg, rg, pterm, gown,
    z_send, z_recv, f_send, f_recv, t_send, t_recv, d_send, d_recv, part, part_recv,
    teach_ss, teach_rs, q_ss, q_rs, z_ss, z_rs, g_ss, g_rs, part_ss, part_rs,
):
    me = lax.axis_index("blk")
    core = lax.rem(me, 2)
    sib = me + 1 - 2 * core
    f32, bf16 = jnp.float32, jnp.bfloat16
    q_rows = queries * q_tokens
    p_rows = p_tokens * passages
    padded = pu.shape[1]
    cand = CYCLE * passages

    def peer(shift):
        return lax.rem(me + shift + n, n)

    def remote(src, dst, ss, rs, target):
        return pltpu.make_async_remote_copy(
            src_ref=src, dst_ref=dst, send_sem=ss, recv_sem=rs,
            device_id={"blk": target}, device_id_type=pl.DeviceIdType.MESH,
        )

    def load(src, dst, at):
        return pltpu.make_async_copy(src, dst, in_sem.at[at])

    width_q = q_rows // PARTS

    def piece(h):
        return slice(h * width_q, (h + 1) * width_q)

    load_proj = load(proj_hbm, proj, 0)
    load_q = [load(qh_hbm.at[piece(h)], qh.at[piece(h)], 1 + h) for h in range(PARTS)]
    load_p = load(ph_hbm, ph, 1 + PARTS)
    small = [(rows_hbm, rows_v), (pos_hbm, pos_v), (cnt_hbm, cnt_v), (len_hbm, len_s)]
    load_small = [load(src, dst, 2 + PARTS + at) for at, (src, dst) in enumerate(small)]
    load_proj.start()
    for copy in load_q:
        copy.start()
    barrier = pltpu.get_barrier_semaphore()

    @pl.loop(1, n)
    def _(k):
        pl.semaphore_signal(
            barrier, inc=1, device_id={"blk": peer(k)}, device_id_type=pl.DeviceIdType.MESH
        )

    for copy in load_small:
        copy.start()

    load_proj.wait()
    proj_t = jnp.transpose(proj[...].astype(f32)).astype(bf16)

    def query_units(h):
        load_q[h].wait()
        raw = dot16(proj_t, qh[piece(h)], NT)
        inv = lax.rsqrt(jnp.sum(raw * raw, axis=0, keepdims=True) + EPSILON)
        qinv[:, piece(h)] = inv
        unit = raw * inv
        qv[:, piece(h)] = unit
        qt[OWN, h] = unit.astype(bf16)

    def q_two(h):
        return remote(qt.at[OWN, h], qt.at[TWO, h], q_ss.at[0, h], q_rs.at[0, h], peer(2))

    def q_direct(h):
        return remote(
            qt.at[OWN, h], qt.at[DIRECT, h], q_ss.at[1, h], q_rs.at[1, h], peer(1 + 2 * core)
        )

    def q_forward(h):
        return remote(qt.at[TWO, h], qt.at[FORWARD, h], q_ss.at[2, h], q_rs.at[2, h], sib)

    query_units(0)
    pl.semaphore_wait(barrier, n - 1)
    q_two(0).start()
    q_direct(0).start()
    for h in range(1, PARTS):
        query_units(h)
        q_two(h).start()
        q_direct(h).start()
    load_p.start()

    for copy in load_small:
        copy.wait()
    per_row = LANES // cand
    deep = queries // per_row
    pos = pos_v[...]
    local = pos % queries
    device = pos // queries
    row = ((device % 2) * (n // 2) + device // 2) * META + local % deep
    chip = me // 2
    teach[core, chip] = jnp.concatenate(
        [jnp.concatenate([rows_v[g * deep : (g + 1) * deep] for g in range(per_row)], axis=1)]
        + [
            jnp.concatenate([x.astype(f32)] * (LANES // queries), axis=1)
            for x in (row, local // deep, cnt_v[...])
        ]
        + [jnp.zeros((META - deep - 3, LANES), f32)],
        axis=0,
    )

    def teach_send(k):
        return remote(
            teach.at[core, chip], teach.at[core, chip], teach_ss.at[k], teach_rs.at[k], peer(2 * k)
        )

    def teach_recv(k):
        return remote(
            teach.at[core, chip], teach.at[core, lax.rem(chip - k + n // 2, n // 2)],
            teach_ss.at[k], teach_rs.at[k], peer(2 * k),
        )

    @pl.loop(1, n // 2)
    def _(k):
        teach_send(k).start()

    teach_across = remote(teach.at[core], teach.at[core], teach_ss.at[0], teach_rs.at[0], sib)
    teach_from = remote(teach.at[core], teach.at[1 - core], teach_ss.at[0], teach_rs.at[0], sib)

    load_p.wait()
    step = p_rows // 6
    for c in range(6):
        at = slice(c * step, (c + 1) * step)
        raw_p = dot16(ph[at], proj[...], NN)
        inv_p = lax.rsqrt(jnp.sum(raw_p * raw_p, axis=1, keepdims=True) + EPSILON)
        tokens = slice(c * step // passages, (c + 1) * step // passages)
        pv[tokens] = (raw_p * inv_p).reshape(step // passages, passages, LANES)
        pinv[at] = jnp.broadcast_to(inv_p, raw_p.shape)
    for p in range(passages):
        x = jnp.concatenate(
            [pv[:, p, :], jnp.zeros((padded - p_tokens, LANES), f32)], axis=0
        )
        pu[p] = x.astype(bf16)
        put[p] = jnp.transpose(x).astype(bf16)

    offset_of = {OWN: 0, TWO: 2, DIRECT: 3 - 2 * core, FORWARD: 1 + 2 * core}
    half = CYCLE * queries
    row_q = lax.broadcasted_iota(jnp.int32, (width_q, LANES), 0) // q_tokens
    lane_q = lax.broadcasted_iota(jnp.int32, (width_q, LANES), 1) % half
    part_q = queries // PARTS
    for h in range(PARTS):
        for slot in range(CYCLE):
            at = h * CYCLE * width_q + slot * width_q
            place[at : at + width_q] = jnp.where(
                lane_q == row_q + offset_of[slot] * queries + h * part_q, 1.0, 0.0
            ).astype(bf16)
    token = lax.broadcasted_iota(jnp.int32, (padded, width_q), 0)

    def lanes(slot, h):
        at = h * CYCLE * width_q + slot * width_q
        return slice(at, at + width_q)

    def half_lanes(h):
        return slice(h * CYCLE * width_q, (h + 1) * CYCLE * width_q)

    def forward(slot, h):
        units = qt[slot, h]
        at = lanes(slot, h)
        for p in range(passages):
            sims = dot16(pu[p], units, NN)
            e = jnp.where(
                token < len_s[0, p], jnp.exp2(sims * (math.log2(math.e) / HEAT)), 0.0
            )
            exps[p, :, at] = e.astype(bf16)
            den[p : p + 1, at] = jnp.sum(e, axis=0, keepdims=True)
        peaks = halves(HEAT * jnp.log(den[:, at]))
        placed = dot16(peaks, place[at], NN)
        return placed[:passages] + placed[passages:]

    def products(slot, h):
        for p in range(passages):
            vs[slot, p, :, piece(h)] = dot16(put[p], exps[p, :, lanes(slot, h)], NN)

    def z_copy(k, h):
        at = CYCLE - 1 - k
        return remote(z_send.at[h], z_recv.at[h, at], z_ss.at[h, at], z_rs.at[h, at], peer(k))

    shifts = [k for k in range(1 - CYCLE, CYCLE) if k]
    own = [forward(OWN, h) for h in range(PARTS)]
    for h in range(PARTS):
        products(OWN, h)

    q_two(0).wait_recv()
    q_forward(0).start()
    students = []
    for h in range(PARTS):
        student = own[h] + forward(TWO, h)
        q_direct(h).wait_recv()
        student = student + forward(DIRECT, h)
        if h + 1 < PARTS:
            q_two(h + 1).wait_recv()
            q_forward(h + 1).start()
        q_forward(h).wait_recv()
        student = student + forward(FORWARD, h)
        students.append(student)
        z_send[h] = student
        for k in shifts:
            z_copy(k, h).start()

    for k in range(1, n // 2):
        teach_recv(k).wait_recv()
    teach_across.start()
    for h in range(PARTS):
        for slot in (TWO, DIRECT, FORWARD):
            products(slot, h)

    group = lax.broadcasted_iota(jnp.int32, (passages, LANES), 1) % half // queries
    low_half = lax.broadcasted_iota(jnp.int32, (passages, LANES), 1) < half
    passage = lax.broadcasted_iota(jnp.int32, (passages, LANES), 0)

    def of_blocks(row):
        value = jnp.zeros((passages, LANES), f32)
        for j in range(CYCLE):
            at = peer(-j)
            theirs = teach[lax.rem(at, 2), at // 2, deep + row : deep + row + 1]
            value = jnp.where(group == j, jnp.broadcast_to(theirs, (passages, LANES)), value)
        return value

    teach_from.wait_recv()
    stored = teach[...].reshape(n * META, LANES)
    counts = of_blocks(2)
    row_at = of_blocks(0)[:1]
    part_at = of_blocks(1)[:1]
    counts_row = counts[:1]
    picks = lax.broadcasted_iota(jnp.int32, (n * META, LANES), 0).astype(f32)
    picked = dot32(stored, jnp.where(picks == row_at, 1.0, 0.0), TN)
    teacher = jnp.zeros((cand, LANES), f32)
    for g in range(per_row):
        teacher = teacher + jnp.where(part_at == g, picked[g * cand : (g + 1) * cand], 0.0)
    ids = lax.broadcasted_iota(jnp.int32, (cand, LANES), 0).astype(f32)
    teacher_exp = jnp.where(ids < counts_row, jnp.exp(teacher), 0.0)
    teacher_total = jnp.sum(teacher_exp, axis=0, keepdims=True)
    all_prob = teacher_exp / teacher_total
    all_log = teacher - jnp.log(teacher_total)
    prob = jnp.zeros((passages, LANES), f32)
    for j in range(CYCLE):
        prob = jnp.where(group == j, all_prob[j * passages : (j + 1) * passages], prob)

    part_of = lax.broadcasted_iota(jnp.int32, (passages, LANES), 1) % queries // part_q

    def valid(k):
        index = ((group + k) * passages + passage).astype(f32)
        return (group + k >= 0) & (group + k < CYCLE) & (index < counts)

    masks = {k: valid(k) for k in shifts}
    mask = valid(0)

    def score_part(h):
        student = students[h]
        es = jnp.where(mask, jnp.exp(student), 0.0)
        all_es = es
        own_scores = [student]
        for k in shifts:
            z_copy(k, h).wait_recv()
        for k in shifts:
            moved = pltpu.roll(z_recv[h, k + CYCLE - 1], (-k * queries) % LANES, 1)
            all_es = all_es + jnp.where(masks[k], jnp.exp(moved), 0.0)
            if k > 0:
                own_scores.append(moved)
        total = jnp.sum(all_es, axis=0, keepdims=True)
        mine = mask & low_half & (part_of == h)
        score_grad = jnp.where(mine, es / total - prob, 0.0)
        spread = dot16(halves(score_grad), place[half_lanes(h)], NT)
        scales[:, half_lanes(h)] = (spread[:passages] + spread[passages:]) / den[:, half_lanes(h)]
        gap = all_log - (jnp.concatenate(own_scores, axis=0) - jnp.log(total))
        return jnp.where(ids < counts_row, all_prob * gap, 0.0)

    def combine(slot, h):
        at = lanes(slot, h)
        out = vs[slot, 0, :, piece(h)] * scales[0:1, at]
        for p in range(1, passages):
            out = out + vs[slot, p, :, piece(h)] * scales[p : p + 1, at]
        return out

    def g_forward(h):
        return remote(f_send.at[h], f_recv.at[h], g_ss.at[0, h], g_rs.at[0, h], sib)

    def g_direct(h):
        return remote(d_send.at[h], d_recv.at[h], g_ss.at[1, h], g_rs.at[1, h], peer(2 * core - 3))

    def g_two(h):
        return remote(t_send.at[h], t_recv.at[h], g_ss.at[2, h], g_rs.at[2, h], peer(-2))

    gaps = []
    for h in range(PARTS):
        gaps.append(score_part(h))
        f_send[h] = combine(FORWARD, h).astype(bf16)
        g_forward(h).start()
        d_send[h] = combine(DIRECT, h).astype(bf16)
        g_direct(h).start()
        two = combine(TWO, h)
        g_forward(h).wait_recv()
        t_send[h] = (two + f_recv[h].astype(f32)).astype(bf16)
        g_two(h).start()
    for h in range(PARTS):
        gown[:, piece(h)] = combine(OWN, h)
    gap = gaps[0]
    which = lax.broadcasted_iota(jnp.int32, (cand, LANES), 1) % queries // part_q
    for h in range(1, PARTS):
        gap = jnp.where(which == h, gaps[h], gap)
    loss = jnp.sum(gap, axis=0, keepdims=True)
    loss_ref[...] = loss[:, :queries]

    for p in range(passages):
        total_p = None
        for slot in range(CYCLE):
            for h in range(PARTS):
                at = lanes(slot, h)
                scaled = (qt[slot, h].astype(f32) * scales[p : p + 1, at]).astype(bf16)
                term = dot16(exps[p, :, at], scaled, NT)
                total_p = term if total_p is None else total_p + term
        pg[:, p, :] = total_p[:p_tokens]
    for c in range(6):
        at = slice(c * step, (c + 1) * step)
        tokens = slice(c * step // passages, (c + 1) * step // passages)
        v = pv[tokens].reshape(step, LANES)
        g = pg[tokens].reshape(step, LANES)
        raw_g = (g - v * jnp.sum(v * g, axis=1, keepdims=True)) * pinv[at]
        rg[at] = raw_g.astype(bf16)
    pterm[...] = dot16(rg[...], ph[...], TN)

    whole = pterm[...]
    for h in range(PARTS):
        g_direct(h).wait_recv()
        g_two(h).wait_recv()
        v = qv[:, piece(h)]
        g = gown[:, piece(h)] + d_recv[h].astype(f32) + t_recv[h].astype(f32)
        raw_g = (g - v * jnp.sum(v * g, axis=0, keepdims=True)) * qinv[:, piece(h)]
        whole = whole + dot16(raw_g.astype(bf16), qh[piece(h)], NN)
    whole = jnp.transpose(whole)
    chunk = grad_ref.shape[0]
    for k in range(n):
        part[k] = whole[k * chunk : (k + 1) * chunk].astype(bf16)

    def part_copy(k):
        return remote(part.at[peer(k)], part_recv.at[k], part_ss.at[k], part_rs.at[k], peer(k))

    @pl.loop(1, n)
    def _(k):
        part_copy(k).start()

    grad_ref[...] = part[me].astype(f32)

    @pl.loop(1, n)
    def _(k):
        part_copy(k).wait_recv()
        grad_ref[...] += part_recv[k].astype(f32)

    for h in range(PARTS):
        q_two(h).wait_send()
        q_direct(h).wait_send()
        q_forward(h).wait_send()
        g_forward(h).wait_send()
        g_direct(h).wait_send()
        g_two(h).wait_send()
    for h in range(PARTS):
        for k in shifts:
            z_copy(k, h).wait_send()
    teach_across.wait_send()

    @pl.loop(1, n // 2)
    def _(k):
        teach_send(k).wait_send()

    @pl.loop(1, n)
    def _(k):
        part_copy(k).wait_send()


def per_device(
    n, query_hidden, passage_hidden, projection, teacher_rows, teacher_pos, neg_count, pass_len
):
    queries, q_tokens, width = query_hidden.shape
    passages, p_tokens, _ = passage_hidden.shape
    dim = projection.shape[1]
    q_rows = queries * q_tokens
    p_rows = passages * p_tokens
    padded = -(-p_tokens // 16) * 16
    chunk = width // n
    f32, bf16, i32 = jnp.float32, jnp.bfloat16, jnp.int32
    vmem = pl.BlockSpec(memory_space=pltpu.VMEM)
    hbm = pl.BlockSpec(memory_space=pltpu.HBM)
    dma = pltpu.SemaphoreType.DMA
    loss, grad_w = pl.pallas_call(
        functools.partial(kernel, n, queries, q_tokens, passages, p_tokens),
        out_shape=(
            jax.ShapeDtypeStruct((1, queries), f32),
            jax.ShapeDtypeStruct((chunk, dim), f32),
        ),
        in_specs=[hbm] * 7,
        out_specs=(vmem, vmem),
        scratch_shapes=[
            pltpu.VMEM((q_rows, width), bf16),
            pltpu.VMEM((p_rows, width), bf16),
            pltpu.VMEM((width, dim), bf16),
            pltpu.VMEM((queries, CYCLE * passages), f32),
            pltpu.VMEM((1, queries), i32),
            pltpu.VMEM((1, queries), i32),
            pltpu.SMEM((1, passages), i32),
            dma((6 + PARTS,)),
            pltpu.VMEM((2, n // 2, META, LANES), f32),
            pltpu.VMEM((dim, q_rows), f32),
            pltpu.VMEM((1, q_rows), f32),
            pltpu.VMEM((CYCLE, PARTS, dim, q_rows // PARTS), bf16),
            pltpu.VMEM((p_tokens, passages, dim), f32),
            pltpu.VMEM((p_rows, dim), f32),
            pltpu.VMEM((passages, padded, dim), bf16),
            pltpu.VMEM((passages, dim, padded), bf16),
            pltpu.VMEM((passages, padded, CYCLE * q_rows), bf16),
            pltpu.VMEM((passages, CYCLE * q_rows), f32),
            pltpu.VMEM((passages, CYCLE * q_rows), f32),
            pltpu.VMEM((CYCLE, passages, dim, q_rows), f32),
            pltpu.VMEM((CYCLE * q_rows, LANES), bf16),
            pltpu.VMEM((p_tokens, passages, dim), f32),
            pltpu.VMEM((p_rows, dim), bf16),
            pltpu.VMEM((dim, width), f32),
            pltpu.VMEM((dim, q_rows), f32),
            pltpu.VMEM((PARTS, passages, LANES), f32),
            pltpu.VMEM((PARTS, 2 * CYCLE - 1, passages, LANES), f32),
        ]
        + [pltpu.VMEM((PARTS, dim, q_rows // PARTS), bf16)] * 6
        + [
            pltpu.VMEM((n, chunk, dim), bf16),
            pltpu.VMEM((n, chunk, dim), bf16),
            dma((n // 2,)), dma((n // 2,)),
            dma((3, PARTS)), dma((3, PARTS)),
            dma((PARTS, 2 * CYCLE - 1)), dma((PARTS, 2 * CYCLE - 1)),
            dma((3, PARTS)), dma((3, PARTS)),
            dma((n,)), dma((n,)),
        ],
        compiler_params=pltpu.CompilerParams(
            collective_id=0, has_side_effects=True, vmem_limit_bytes=50 * 1024 * 1024
        ),
    )(
        *[
            pltpu.with_memory_space_constraint(x, pltpu.HBM)
            for x in (
                query_hidden.reshape(q_rows, width),
                jnp.transpose(passage_hidden, (1, 0, 2)).reshape(p_rows, width),
                projection,
                teacher_rows,
                teacher_pos.reshape(1, queries),
                neg_count.reshape(1, queries),
                pass_len.reshape(1, passages),
            )
        ]
    )
    def results(loss_in, grad_in, loss_out, grad_out, sem):
        first = pltpu.make_async_copy(loss_in, loss_out, sem.at[0])
        second = pltpu.make_async_copy(grad_in, grad_out, sem.at[1])
        first.start()
        second.start()
        first.wait()
        second.wait()

    loss, grad_w = pl.pallas_call(
        results,
        out_shape=(
            jax.ShapeDtypeStruct((1, queries), f32),
            jax.ShapeDtypeStruct((chunk, dim), f32),
        ),
        in_specs=[vmem, vmem],
        out_specs=(hbm, hbm),
        scratch_shapes=[dma((2,))],
        compiler_params=pltpu.CompilerParams(vmem_limit_bytes=1024 * 1024),
    )(loss, grad_w)
    return (loss.reshape(queries), grad_w)


def solution(mesh):
    return jax.shard_map(
        functools.partial(per_device, mesh.shape["blk"]),
        mesh=mesh,
        in_specs=(
            P(("groups", "blk"), None, None),
            P(("groups", "blk"), None, None),
            P(),
            P(("groups", "blk"), None),
            P(("groups", "blk")),
            P(("groups", "blk")),
            P(("groups", "blk")),
        ),
        out_specs=(P(("groups", "blk")), P(("groups", "blk"), None)),
        check_vma=False,
    )
```

```python
import functools
import math

import jax
import jax.numpy as jnp
from jax import lax
from jax.experimental import pallas as pl
from jax.experimental.pallas import tpu as pltpu
from jax.sharding import PartitionSpec as P

CYCLE = 4
HEAT = 0.05
EPSILON = 1e-06
LANES = 128
META = 8
PARTS = 2
NN = (((1,), (0,)), ((), ()))
NT = (((1,), (1,)), ((), ()))
TN = (((0,), (0,)), ((), ()))
OWN, TWO, DIRECT, FORWARD = range(4)


def dot16(a, b, dims):
    return lax.dot_general(a, b, dims, preferred_element_type=jnp.float32)


def dot32(a, b, dims):
    return lax.dot_general(
        a, b, dims, precision=lax.Precision.HIGHEST, preferred_element_type=jnp.float32
    )


def halves(x):
    high = x.astype(jnp.bfloat16)
    low = (x - high.astype(jnp.float32)).astype(jnp.bfloat16)
    return jnp.concatenate([high, low], axis=0)


def kernel(
    n, queries, q_tokens, passages, p_tokens,
    qh_hbm, ph_hbm, proj_hbm, rows_hbm, pos_hbm, cnt_hbm, len_hbm,
    loss_ref, grad_ref,
    qh, ph, proj, rows_v, pos_v, cnt_v, len_s, in_sem,
    teach, qv, qinv, qt, pv, pinv, pu, put, exps, den, scales, vs, place, pg, rg, pterm, gown,
    z_send, z_recv, f_send, f_recv, t_send, t_recv, d_send, d_recv, part, part_recv,
    teach_ss, teach_rs, q_ss, q_rs, z_ss, z_rs, g_ss, g_rs, part_ss, part_rs,
):
    me = lax.axis_index("blk")
    core = lax.rem(me, 2)
    sib = me + 1 - 2 * core
    f32, bf16 = jnp.float32, jnp.bfloat16
    q_rows = queries * q_tokens
    p_rows = p_tokens * passages
    padded = pu.shape[1]
    cand = CYCLE * passages

    def peer(shift):
        return lax.rem(me + shift + n, n)

    def remote(src, dst, ss, rs, target):
        return pltpu.make_async_remote_copy(
            src_ref=src, dst_ref=dst, send_sem=ss, recv_sem=rs,
            device_id={"blk": target}, device_id_type=pl.DeviceIdType.MESH,
        )

    def load(src, dst, at):
        return pltpu.make_async_copy(src, dst, in_sem.at[at])

    width_q = q_rows // PARTS

    def piece(h):
        return slice(h * width_q, (h + 1) * width_q)

    load_proj = load(proj_hbm, proj, 0)
    load_q = [load(qh_hbm.at[piece(h)], qh.at[piece(h)], 1 + h) for h in range(PARTS)]
    load_p = load(ph_hbm, ph, 1 + PARTS)
    small = [(rows_hbm, rows_v), (pos_hbm, pos_v), (cnt_hbm, cnt_v), (len_hbm, len_s)]
    load_small = [load(src, dst, 2 + PARTS + at) for at, (src, dst) in enumerate(small)]
    load_proj.start()
    for copy in load_q:
        copy.start()
    barrier = pltpu.get_barrier_semaphore()

    @pl.loop(1, n)
    def _(k):
        pl.semaphore_signal(
            barrier, inc=1, device_id={"blk": peer(k)}, device_id_type=pl.DeviceIdType.MESH
        )

    for copy in load_small:
        copy.start()

    load_proj.wait()
    proj_t = jnp.transpose(proj[...].astype(f32)).astype(bf16)

    def query_units(h):
        load_q[h].wait()
        raw = dot16(proj_t, qh[piece(h)], NT)
        inv = lax.rsqrt(jnp.sum(raw * raw, axis=0, keepdims=True) + EPSILON)
        qinv[:, piece(h)] = inv
        unit = raw * inv
        qv[:, piece(h)] = unit
        qt[OWN, h] = unit.astype(bf16)

    def q_two(h):
        return remote(qt.at[OWN, h], qt.at[TWO, h], q_ss.at[0, h], q_rs.at[0, h], peer(2))

    def q_direct(h):
        return remote(
            qt.at[OWN, h], qt.at[DIRECT, h], q_ss.at[1, h], q_rs.at[1, h], peer(1 + 2 * core)
        )

    def q_forward(h):
        return remote(qt.at[TWO, h], qt.at[FORWARD, h], q_ss.at[2, h], q_rs.at[2, h], sib)

    query_units(0)
    pl.semaphore_wait(barrier, n - 1)
    q_two(0).start()
    q_direct(0).start()
    for h in range(1, PARTS):
        query_units(h)
        q_two(h).start()
        q_direct(h).start()
    load_p.start()

    for copy in load_small:
        copy.wait()
    per_row = LANES // cand
    deep = queries // per_row
    pos = pos_v[...]
    local = pos % queries
    device = pos // queries
    row = ((device % 2) * (n // 2) + device // 2) * META + local % deep
    chip = me // 2
    teach[core, chip] = jnp.concatenate(
        [jnp.concatenate([rows_v[g * deep : (g + 1) * deep] for g in range(per_row)], axis=1)]
        + [
            jnp.concatenate([x.astype(f32)] * (LANES // queries), axis=1)
            for x in (row, local // deep, cnt_v[...])
        ]
        + [jnp.zeros((META - deep - 3, LANES), f32)],
        axis=0,
    )

    def teach_send(k):
        return remote(
            teach.at[core, chip], teach.at[core, chip], teach_ss.at[k], teach_rs.at[k], peer(2 * k)
        )

    def teach_recv(k):
        return remote(
            teach.at[core, chip], teach.at[core, lax.rem(chip - k + n // 2, n // 2)],
            teach_ss.at[k], teach_rs.at[k], peer(2 * k),
        )

    teach_across = remote(teach.at[core], teach.at[core], teach_ss.at[0], teach_rs.at[0], sib)
    teach_from = remote(teach.at[core], teach.at[1 - core], teach_ss.at[0], teach_rs.at[0], sib)

    load_p.wait()
    step = p_rows // 6
    for c in range(6):
        at = slice(c * step, (c + 1) * step)
        raw_p = dot16(ph[at], proj[...], NN)
        inv_p = lax.rsqrt(jnp.sum(raw_p * raw_p, axis=1, keepdims=True) + EPSILON)
        tokens = slice(c * step // passages, (c + 1) * step // passages)
        pv[tokens] = (raw_p * inv_p).reshape(step // passages, passages, LANES)
        pinv[at] = jnp.broadcast_to(inv_p, raw_p.shape)
    for p in range(passages):
        x = jnp.concatenate(
            [pv[:, p, :], jnp.zeros((padded - p_tokens, LANES), f32)], axis=0
        )
        pu[p] = x.astype(bf16)
        put[p] = jnp.transpose(x).astype(bf16)

    offset_of = {OWN: 0, TWO: 2, DIRECT: 3 - 2 * core, FORWARD: 1 + 2 * core}
    half = CYCLE * queries
    row_q = lax.broadcasted_iota(jnp.int32, (width_q, LANES), 0) // q_tokens
    lane_q = lax.broadcasted_iota(jnp.int32, (width_q, LANES), 1) % half
    part_q = queries // PARTS
    for h in range(PARTS):
        for slot in range(CYCLE):
            at = h * CYCLE * width_q + slot * width_q
            place[at : at + width_q] = jnp.where(
                lane_q == row_q + offset_of[slot] * queries + h * part_q, 1.0, 0.0
            ).astype(bf16)
    token = lax.broadcasted_iota(jnp.int32, (padded, width_q), 0)

    def lanes(slot, h):
        at = h * CYCLE * width_q + slot * width_q
        return slice(at, at + width_q)

    def half_lanes(h):
        return slice(h * CYCLE * width_q, (h + 1) * CYCLE * width_q)

    def forward(slot, h):
        units = qt[slot, h]
        at = lanes(slot, h)
        for p in range(passages):
            sims = dot16(pu[p], units, NN)
            e = jnp.where(
                token < len_s[0, p], jnp.exp2(sims * (math.log2(math.e) / HEAT)), 0.0
            )
            exps[p, :, at] = e.astype(bf16)
            den[p : p + 1, at] = jnp.sum(e, axis=0, keepdims=True)
        peaks = halves(HEAT * jnp.log(den[:, at]))
        placed = dot16(peaks, place[at], NN)
        return placed[:passages] + placed[passages:]

    def products(slot, h):
        for p in range(passages):
            vs[slot, p, :, piece(h)] = dot16(put[p], exps[p, :, lanes(slot, h)], NN)

    def z_copy(k, h):
        at = CYCLE - 1 - k
        return remote(z_send.at[h], z_recv.at[h, at], z_ss.at[h, at], z_rs.at[h, at], peer(k))

    shifts = [k for k in range(1 - CYCLE, CYCLE) if k]
    own = [forward(OWN, h) for h in range(PARTS)]
    for h in range(PARTS):
        products(OWN, h)

    q_two(0).wait_recv()
    q_forward(0).start()

    @pl.loop(1, n // 2)
    def _(k):
        teach_send(k).start()

    students = []
    for h in range(PARTS):
        student = own[h] + forward(TWO, h)
        q_direct(h).wait_recv()
        student = student + forward(DIRECT, h)
        if h + 1 < PARTS:
            q_two(h + 1).wait_recv()
            q_forward(h + 1).start()
        q_forward(h).wait_recv()
        student = student + forward(FORWARD, h)
        students.append(student)
        z_send[h] = student
        for k in shifts:
            z_copy(k, h).start()

    for k in range(1, n // 2):
        teach_recv(k).wait_recv()
    teach_across.start()
    for h in range(PARTS):
        for slot in (TWO, DIRECT, FORWARD):
            products(slot, h)

    group = lax.broadcasted_iota(jnp.int32, (passages, LANES), 1) % half // queries
    low_half = lax.broadcasted_iota(jnp.int32, (passages, LANES), 1) < half
    passage = lax.broadcasted_iota(jnp.int32, (passages, LANES), 0)

    def of_blocks(row):
        value = jnp.zeros((passages, LANES), f32)
        for j in range(CYCLE):
            at = peer(-j)
            theirs = teach[lax.rem(at, 2), at // 2, deep + row : deep + row + 1]
            value = jnp.where(group == j, jnp.broadcast_to(theirs, (passages, LANES)), value)
        return value

    teach_from.wait_recv()
    stored = teach[...].reshape(n * META, LANES)
    counts = of_blocks(2)
    row_at = of_blocks(0)[:1]
    part_at = of_blocks(1)[:1]
    counts_row = counts[:1]
    picks = lax.broadcasted_iota(jnp.int32, (n * META, LANES), 0).astype(f32)
    picked = dot32(stored, jnp.where(picks == row_at, 1.0, 0.0), TN)
    teacher = jnp.zeros((cand, LANES), f32)
    for g in range(per_row):
        teacher = teacher + jnp.where(part_at == g, picked[g * cand : (g + 1) * cand], 0.0)
    ids = lax.broadcasted_iota(jnp.int32, (cand, LANES), 0).astype(f32)
    teacher_exp = jnp.where(ids < counts_row, jnp.exp(teacher), 0.0)
    teacher_total = jnp.sum(teacher_exp, axis=0, keepdims=True)
    all_prob = teacher_exp / teacher_total
    all_log = teacher - jnp.log(teacher_total)
    prob = jnp.zeros((passages, LANES), f32)
    for j in range(CYCLE):
        prob = jnp.where(group == j, all_prob[j * passages : (j + 1) * passages], prob)

    part_of = lax.broadcasted_iota(jnp.int32, (passages, LANES), 1) % queries // part_q

    def valid(k):
        index = ((group + k) * passages + passage).astype(f32)
        return (group + k >= 0) & (group + k < CYCLE) & (index < counts)

    masks = {k: valid(k) for k in shifts}
    mask = valid(0)

    def score_part(h):
        student = students[h]
        es = jnp.where(mask, jnp.exp(student), 0.0)
        all_es = es
        own_scores = [student]
        for k in shifts:
            z_copy(k, h).wait_recv()
        for k in shifts:
            moved = pltpu.roll(z_recv[h, k + CYCLE - 1], (-k * queries) % LANES, 1)
            all_es = all_es + jnp.where(masks[k], jnp.exp(moved), 0.0)
            if k > 0:
                own_scores.append(moved)
        total = jnp.sum(all_es, axis=0, keepdims=True)
        mine = mask & low_half & (part_of == h)
        score_grad = jnp.where(mine, es / total - prob, 0.0)
        spread = dot16(halves(score_grad), place[half_lanes(h)], NT)
        scales[:, half_lanes(h)] = (spread[:passages] + spread[passages:]) / den[:, half_lanes(h)]
        gap = all_log - (jnp.concatenate(own_scores, axis=0) - jnp.log(total))
        return jnp.where(ids < counts_row, all_prob * gap, 0.0)

    def combine(slot, h):
        at = lanes(slot, h)
        out = vs[slot, 0, :, piece(h)] * scales[0:1, at]
        for p in range(1, passages):
            out = out + vs[slot, p, :, piece(h)] * scales[p : p + 1, at]
        return out

    def g_forward(h):
        return remote(f_send.at[h], f_recv.at[h], g_ss.at[0, h], g_rs.at[0, h], sib)

    def g_direct(h):
        return remote(d_send.at[h], d_recv.at[h], g_ss.at[1, h], g_rs.at[1, h], peer(2 * core - 3))

    def g_two(h):
        return remote(t_send.at[h], t_recv.at[h], g_ss.at[2, h], g_rs.at[2, h], peer(-2))

    gaps = []
    for h in range(PARTS):
        gaps.append(score_part(h))
        f_send[h] = combine(FORWARD, h).astype(bf16)
        g_forward(h).start()
        d_send[h] = combine(DIRECT, h).astype(bf16)
        g_direct(h).start()
        two = combine(TWO, h)
        g_forward(h).wait_recv()
        t_send[h] = (two + f_recv[h].astype(f32)).astype(bf16)
        g_two(h).start()
    for h in range(PARTS):
        gown[:, piece(h)] = combine(OWN, h)
    gap = gaps[0]
    which = lax.broadcasted_iota(jnp.int32, (cand, LANES), 1) % queries // part_q
    for h in range(1, PARTS):
        gap = jnp.where(which == h, gaps[h], gap)
    loss = jnp.sum(gap, axis=0, keepdims=True)
    loss_ref[...] = loss[:, :queries]

    for p in range(passages):
        total_p = None
        for slot in range(CYCLE):
            for h in range(PARTS):
                at = lanes(slot, h)
                scaled = (qt[slot, h].astype(f32) * scales[p : p + 1, at]).astype(bf16)
                term = dot16(exps[p, :, at], scaled, NT)
                total_p = term if total_p is None else total_p + term
        pg[:, p, :] = total_p[:p_tokens]
    for c in range(6):
        at = slice(c * step, (c + 1) * step)
        tokens = slice(c * step // passages, (c + 1) * step // passages)
        v = pv[tokens].reshape(step, LANES)
        g = pg[tokens].reshape(step, LANES)
        raw_g = (g - v * jnp.sum(v * g, axis=1, keepdims=True)) * pinv[at]
        rg[at] = raw_g.astype(bf16)
    pterm[...] = dot16(rg[...], ph[...], TN)

    whole = pterm[...]
    for h in range(PARTS):
        g_direct(h).wait_recv()
        g_two(h).wait_recv()
        v = qv[:, piece(h)]
        g = gown[:, piece(h)] + d_recv[h].astype(f32) + t_recv[h].astype(f32)
        raw_g = (g - v * jnp.sum(v * g, axis=0, keepdims=True)) * qinv[:, piece(h)]
        whole = whole + dot16(raw_g.astype(bf16), qh[piece(h)], NN)
    whole = jnp.transpose(whole)
    chunk = grad_ref.shape[0]
    for k in range(n):
        part[k] = whole[k * chunk : (k + 1) * chunk].astype(bf16)

    def part_copy(k):
        return remote(part.at[peer(k)], part_recv.at[k], part_ss.at[k], part_rs.at[k], peer(k))

    @pl.loop(0, n)
    def _(i):
        t = i // 2 * 2 + lax.rem(i + me, 2)

        @pl.when(me != t)
        def _():
            part_copy(lax.rem(t - me + n, n)).start()

    grad_ref[...] = part[me].astype(f32)

    @pl.loop(1, n)
    def _(k):
        part_copy(k).wait_recv()
        grad_ref[...] += part_recv[k].astype(f32)

    for h in range(PARTS):
        q_two(h).wait_send()
        q_direct(h).wait_send()
        q_forward(h).wait_send()
        g_forward(h).wait_send()
        g_direct(h).wait_send()
        g_two(h).wait_send()
    for h in range(PARTS):
        for k in shifts:
            z_copy(k, h).wait_send()
    teach_across.wait_send()

    @pl.loop(1, n // 2)
    def _(k):
        teach_send(k).wait_send()

    @pl.loop(1, n)
    def _(k):
        part_copy(k).wait_send()


def per_device(
    n, query_hidden, passage_hidden, projection, teacher_rows, teacher_pos, neg_count, pass_len
):
    queries, q_tokens, width = query_hidden.shape
    passages, p_tokens, _ = passage_hidden.shape
    dim = projection.shape[1]
    q_rows = queries * q_tokens
    p_rows = passages * p_tokens
    padded = -(-p_tokens // 16) * 16
    chunk = width // n
    f32, bf16, i32 = jnp.float32, jnp.bfloat16, jnp.int32
    vmem = pl.BlockSpec(memory_space=pltpu.VMEM)
    hbm = pl.BlockSpec(memory_space=pltpu.HBM)
    dma = pltpu.SemaphoreType.DMA
    loss, grad_w = pl.pallas_call(
        functools.partial(kernel, n, queries, q_tokens, passages, p_tokens),
        out_shape=(
            jax.ShapeDtypeStruct((1, queries), f32),
            jax.ShapeDtypeStruct((chunk, dim), f32),
        ),
        in_specs=[hbm] * 7,
        out_specs=(vmem, vmem),
        scratch_shapes=[
            pltpu.VMEM((q_rows, width), bf16),
            pltpu.VMEM((p_rows, width), bf16),
            pltpu.VMEM((width, dim), bf16),
            pltpu.VMEM((queries, CYCLE * passages), f32),
            pltpu.VMEM((1, queries), i32),
            pltpu.VMEM((1, queries), i32),
            pltpu.SMEM((1, passages), i32),
            dma((6 + PARTS,)),
            pltpu.VMEM((2, n // 2, META, LANES), f32),
            pltpu.VMEM((dim, q_rows), f32),
            pltpu.VMEM((1, q_rows), f32),
            pltpu.VMEM((CYCLE, PARTS, dim, q_rows // PARTS), bf16),
            pltpu.VMEM((p_tokens, passages, dim), f32),
            pltpu.VMEM((p_rows, dim), f32),
            pltpu.VMEM((passages, padded, dim), bf16),
            pltpu.VMEM((passages, dim, padded), bf16),
            pltpu.VMEM((passages, padded, CYCLE * q_rows), bf16),
            pltpu.VMEM((passages, CYCLE * q_rows), f32),
            pltpu.VMEM((passages, CYCLE * q_rows), f32),
            pltpu.VMEM((CYCLE, passages, dim, q_rows), f32),
            pltpu.VMEM((CYCLE * q_rows, LANES), bf16),
            pltpu.VMEM((p_tokens, passages, dim), f32),
            pltpu.VMEM((p_rows, dim), bf16),
            pltpu.VMEM((dim, width), f32),
            pltpu.VMEM((dim, q_rows), f32),
            pltpu.VMEM((PARTS, passages, LANES), f32),
            pltpu.VMEM((PARTS, 2 * CYCLE - 1, passages, LANES), f32),
        ]
        + [pltpu.VMEM((PARTS, dim, q_rows // PARTS), bf16)] * 6
        + [
            pltpu.VMEM((n, chunk, dim), bf16),
            pltpu.VMEM((n, chunk, dim), bf16),
            dma((n // 2,)), dma((n // 2,)),
            dma((3, PARTS)), dma((3, PARTS)),
            dma((PARTS, 2 * CYCLE - 1)), dma((PARTS, 2 * CYCLE - 1)),
            dma((3, PARTS)), dma((3, PARTS)),
            dma((n,)), dma((n,)),
        ],
        compiler_params=pltpu.CompilerParams(
            collective_id=0, has_side_effects=True, vmem_limit_bytes=50 * 1024 * 1024
        ),
    )(
        *[
            pltpu.with_memory_space_constraint(x, pltpu.HBM)
            for x in (
                query_hidden.reshape(q_rows, width),
                jnp.transpose(passage_hidden, (1, 0, 2)).reshape(p_rows, width),
                projection,
                teacher_rows,
                teacher_pos.reshape(1, queries),
                neg_count.reshape(1, queries),
                pass_len.reshape(1, passages),
            )
        ]
    )
    def results(loss_in, grad_in, loss_out, grad_out, sem):
        first = pltpu.make_async_copy(loss_in, loss_out, sem.at[0])
        second = pltpu.make_async_copy(grad_in, grad_out, sem.at[1])
        first.start()
        second.start()
        first.wait()
        second.wait()

    loss, grad_w = pl.pallas_call(
        results,
        out_shape=(
            jax.ShapeDtypeStruct((1, queries), f32),
            jax.ShapeDtypeStruct((chunk, dim), f32),
        ),
        in_specs=[vmem, vmem],
        out_specs=(hbm, hbm),
        scratch_shapes=[dma((2,))],
        compiler_params=pltpu.CompilerParams(vmem_limit_bytes=1024 * 1024),
    )(loss, grad_w)
    return (loss.reshape(queries), grad_w)


def solution(mesh):
    return jax.shard_map(
        functools.partial(per_device, mesh.shape["blk"]),
        mesh=mesh,
        in_specs=(
            P(("groups", "blk"), None, None),
            P(("groups", "blk"), None, None),
            P(),
            P(("groups", "blk"), None),
            P(("groups", "blk")),
            P(("groups", "blk")),
            P(("groups", "blk")),
        ),
        out_specs=(P(("groups", "blk")), P(("groups", "blk"), None)),
        check_vma=False,
    )
```

```python
import functools
import math

import jax
import jax.numpy as jnp
from jax import lax
from jax.experimental import pallas as pl
from jax.experimental.pallas import tpu as pltpu
from jax.sharding import PartitionSpec as P

CYCLE = 4
HEAT = 0.05
EPSILON = 1e-06
LANES = 128
META = 8
PARTS = 2
NN = (((1,), (0,)), ((), ()))
NT = (((1,), (1,)), ((), ()))
TN = (((0,), (0,)), ((), ()))
OWN, TWO, DIRECT, FORWARD = range(4)


def dot16(a, b, dims):
    return lax.dot_general(a, b, dims, preferred_element_type=jnp.float32)


def dot32(a, b, dims):
    return lax.dot_general(
        a, b, dims, precision=lax.Precision.HIGHEST, preferred_element_type=jnp.float32
    )


def halves(x):
    high = x.astype(jnp.bfloat16)
    low = (x - high.astype(jnp.float32)).astype(jnp.bfloat16)
    return jnp.concatenate([high, low], axis=0)


def kernel(
    n, queries, q_tokens, passages, p_tokens,
    qh_hbm, ph_hbm, proj_hbm, rows_hbm, pos_hbm, cnt_hbm, len_hbm,
    loss_ref, grad_ref,
    qh, ph, proj, rows_v, pos_v, cnt_v, len_s, in_sem,
    teach, qv, qinv, qt, pv, pinv, pu, put, exps, den, scales, vs, place, pg, rg, pterm, gown,
    z_send, z_recv, f_send, f_recv, t_send, t_recv, d_send, d_recv, part, part_recv,
    teach_ss, teach_rs, q_ss, q_rs, z_ss, z_rs, g_ss, g_rs, part_ss, part_rs,
):
    me = lax.axis_index("blk")
    core = lax.rem(me, 2)
    sib = me + 1 - 2 * core
    f32, bf16 = jnp.float32, jnp.bfloat16
    q_rows = queries * q_tokens
    p_rows = p_tokens * passages
    padded = pu.shape[1]
    cand = CYCLE * passages

    def peer(shift):
        return lax.rem(me + shift + n, n)

    def remote(src, dst, ss, rs, target):
        return pltpu.make_async_remote_copy(
            src_ref=src, dst_ref=dst, send_sem=ss, recv_sem=rs,
            device_id={"blk": target}, device_id_type=pl.DeviceIdType.MESH,
        )

    def load(src, dst, at):
        return pltpu.make_async_copy(src, dst, in_sem.at[at])

    width_q = q_rows // PARTS

    def piece(h):
        return slice(h * width_q, (h + 1) * width_q)

    load_proj = load(proj_hbm, proj, 0)
    load_q = [load(qh_hbm.at[piece(h)], qh.at[piece(h)], 1 + h) for h in range(PARTS)]
    load_p = load(ph_hbm, ph, 1 + PARTS)
    small = [(rows_hbm, rows_v), (pos_hbm, pos_v), (cnt_hbm, cnt_v), (len_hbm, len_s)]
    load_small = [load(src, dst, 2 + PARTS + at) for at, (src, dst) in enumerate(small)]
    load_q[0].start()
    load_proj.start()
    for copy in load_q[1:]:
        copy.start()
    barrier = pltpu.get_barrier_semaphore()

    @pl.loop(1, n)
    def _(k):
        pl.semaphore_signal(
            barrier, inc=1, device_id={"blk": peer(k)}, device_id_type=pl.DeviceIdType.MESH
        )

    for copy in load_small:
        copy.start()

    load_proj.wait()
    proj_t = jnp.transpose(proj[...].astype(f32)).astype(bf16)

    def query_units(h):
        load_q[h].wait()
        raw = dot16(proj_t, qh[piece(h)], NT)
        inv = lax.rsqrt(jnp.sum(raw * raw, axis=0, keepdims=True) + EPSILON)
        qinv[:, piece(h)] = inv
        unit = raw * inv
        qv[:, piece(h)] = unit
        qt[OWN, h] = unit.astype(bf16)

    def q_two(h):
        return remote(qt.at[OWN, h], qt.at[TWO, h], q_ss.at[0, h], q_rs.at[0, h], peer(2))

    def q_direct(h):
        return remote(
            qt.at[OWN, h], qt.at[DIRECT, h], q_ss.at[1, h], q_rs.at[1, h], peer(1 + 2 * core)
        )

    def q_forward(h):
        return remote(qt.at[TWO, h], qt.at[FORWARD, h], q_ss.at[2, h], q_rs.at[2, h], sib)

    query_units(0)
    pl.semaphore_wait(barrier, n - 1)
    q_two(0).start()
    q_direct(0).start()
    for h in range(1, PARTS):
        query_units(h)
        q_two(h).start()
        q_direct(h).start()
    load_p.start()

    for copy in load_small:
        copy.wait()
    per_row = LANES // cand
    deep = queries // per_row
    pos = pos_v[...]
    local = pos % queries
    device = pos // queries
    row = ((device % 2) * (n // 2) + device // 2) * META + local % deep
    chip = me // 2
    teach[core, chip] = jnp.concatenate(
        [jnp.concatenate([rows_v[g * deep : (g + 1) * deep] for g in range(per_row)], axis=1)]
        + [
            jnp.concatenate([x.astype(f32)] * (LANES // queries), axis=1)
            for x in (row, local // deep, cnt_v[...])
        ]
        + [jnp.zeros((META - deep - 3, LANES), f32)],
        axis=0,
    )

    def teach_send(k):
        return remote(
            teach.at[core, chip], teach.at[core, chip], teach_ss.at[k], teach_rs.at[k], peer(2 * k)
        )

    def teach_recv(k):
        return remote(
            teach.at[core, chip], teach.at[core, lax.rem(chip - k + n // 2, n // 2)],
            teach_ss.at[k], teach_rs.at[k], peer(2 * k),
        )

    teach_across = remote(teach.at[core], teach.at[core], teach_ss.at[0], teach_rs.at[0], sib)
    teach_from = remote(teach.at[core], teach.at[1 - core], teach_ss.at[0], teach_rs.at[0], sib)

    load_p.wait()
    step = p_rows // 6
    for c in range(6):
        at = slice(c * step, (c + 1) * step)
        raw_p = dot16(ph[at], proj[...], NN)
        inv_p = lax.rsqrt(jnp.sum(raw_p * raw_p, axis=1, keepdims=True) + EPSILON)
        tokens = slice(c * step // passages, (c + 1) * step // passages)
        pv[tokens] = (raw_p * inv_p).reshape(step // passages, passages, LANES)
        pinv[at] = jnp.broadcast_to(inv_p, raw_p.shape)
    for p in range(passages):
        x = jnp.concatenate(
            [pv[:, p, :], jnp.zeros((padded - p_tokens, LANES), f32)], axis=0
        )
        pu[p] = x.astype(bf16)
        put[p] = jnp.transpose(x).astype(bf16)

    offset_of = {OWN: 0, TWO: 2, DIRECT: 3 - 2 * core, FORWARD: 1 + 2 * core}
    half = CYCLE * queries
    row_q = lax.broadcasted_iota(jnp.int32, (width_q, LANES), 0) // q_tokens
    lane_q = lax.broadcasted_iota(jnp.int32, (width_q, LANES), 1) % half
    part_q = queries // PARTS
    for h in range(PARTS):
        for slot in range(CYCLE):
            at = h * CYCLE * width_q + slot * width_q
            place[at : at + width_q] = jnp.where(
                lane_q == row_q + offset_of[slot] * queries + h * part_q, 1.0, 0.0
            ).astype(bf16)
    token = lax.broadcasted_iota(jnp.int32, (padded, width_q), 0)

    def lanes(slot, h):
        at = h * CYCLE * width_q + slot * width_q
        return slice(at, at + width_q)

    def half_lanes(h):
        return slice(h * CYCLE * width_q, (h + 1) * CYCLE * width_q)

    def forward(slot, h):
        units = qt[slot, h]
        at = lanes(slot, h)
        for p in range(passages):
            sims = dot16(pu[p], units, NN)
            e = jnp.where(
                token < len_s[0, p], jnp.exp2(sims * (math.log2(math.e) / HEAT)), 0.0
            )
            exps[p, :, at] = e.astype(bf16)
            den[p : p + 1, at] = jnp.sum(e, axis=0, keepdims=True)
        peaks = halves(HEAT * jnp.log(den[:, at]))
        placed = dot16(peaks, place[at], NN)
        return placed[:passages] + placed[passages:]

    def products(slot, h):
        for p in range(passages):
            vs[slot, p, :, piece(h)] = dot16(put[p], exps[p, :, lanes(slot, h)], NN)

    def z_copy(k, h):
        at = CYCLE - 1 - k
        return remote(z_send.at[h], z_recv.at[h, at], z_ss.at[h, at], z_rs.at[h, at], peer(k))

    shifts = [k for k in range(1 - CYCLE, CYCLE) if k]
    own = [forward(OWN, h) for h in range(PARTS)]
    for h in range(PARTS):
        products(OWN, h)

    q_two(0).wait_recv()
    q_forward(0).start()

    @pl.loop(1, n // 2)
    def _(k):
        teach_send(k).start()

    students = []
    for h in range(PARTS):
        student = own[h] + forward(TWO, h)
        q_direct(h).wait_recv()
        student = student + forward(DIRECT, h)
        if h + 1 < PARTS:
            q_two(h + 1).wait_recv()
            q_forward(h + 1).start()
        q_forward(h).wait_recv()
        student = student + forward(FORWARD, h)
        students.append(student)
        z_send[h] = student
        for k in shifts:
            z_copy(k, h).start()

    for k in range(1, n // 2):
        teach_recv(k).wait_recv()
    teach_across.start()
    for h in range(PARTS):
        for slot in (TWO, DIRECT, FORWARD):
            products(slot, h)

    group = lax.broadcasted_iota(jnp.int32, (passages, LANES), 1) % half // queries
    low_half = lax.broadcasted_iota(jnp.int32, (passages, LANES), 1) < half
    passage = lax.broadcasted_iota(jnp.int32, (passages, LANES), 0)

    def of_blocks(row):
        value = jnp.zeros((passages, LANES), f32)
        for j in range(CYCLE):
            at = peer(-j)
            theirs = teach[lax.rem(at, 2), at // 2, deep + row : deep + row + 1]
            value = jnp.where(group == j, jnp.broadcast_to(theirs, (passages, LANES)), value)
        return value

    teach_from.wait_recv()
    stored = teach[...].reshape(n * META, LANES)
    counts = of_blocks(2)
    row_at = of_blocks(0)[:1]
    part_at = of_blocks(1)[:1]
    counts_row = counts[:1]
    picks = lax.broadcasted_iota(jnp.int32, (n * META, LANES), 0).astype(f32)
    picked = dot32(stored, jnp.where(picks == row_at, 1.0, 0.0), TN)
    teacher = jnp.zeros((cand, LANES), f32)
    for g in range(per_row):
        teacher = teacher + jnp.where(part_at == g, picked[g * cand : (g + 1) * cand], 0.0)
    ids = lax.broadcasted_iota(jnp.int32, (cand, LANES), 0).astype(f32)
    teacher_exp = jnp.where(ids < counts_row, jnp.exp(teacher), 0.0)
    teacher_total = jnp.sum(teacher_exp, axis=0, keepdims=True)
    all_prob = teacher_exp / teacher_total
    all_log = teacher - jnp.log(teacher_total)
    prob = jnp.zeros((passages, LANES), f32)
    for j in range(CYCLE):
        prob = jnp.where(group == j, all_prob[j * passages : (j + 1) * passages], prob)

    part_of = lax.broadcasted_iota(jnp.int32, (passages, LANES), 1) % queries // part_q

    def valid(k):
        index = ((group + k) * passages + passage).astype(f32)
        return (group + k >= 0) & (group + k < CYCLE) & (index < counts)

    masks = {k: valid(k) for k in shifts}
    mask = valid(0)

    def score_part(h):
        student = students[h]
        es = jnp.where(mask, jnp.exp(student), 0.0)
        all_es = es
        own_scores = [student]
        for k in shifts:
            z_copy(k, h).wait_recv()
        for k in shifts:
            moved = pltpu.roll(z_recv[h, k + CYCLE - 1], (-k * queries) % LANES, 1)
            all_es = all_es + jnp.where(masks[k], jnp.exp(moved), 0.0)
            if k > 0:
                own_scores.append(moved)
        total = jnp.sum(all_es, axis=0, keepdims=True)
        mine = mask & low_half & (part_of == h)
        score_grad = jnp.where(mine, es / total - prob, 0.0)
        spread = dot16(halves(score_grad), place[half_lanes(h)], NT)
        scales[:, half_lanes(h)] = (spread[:passages] + spread[passages:]) / den[:, half_lanes(h)]
        gap = all_log - (jnp.concatenate(own_scores, axis=0) - jnp.log(total))
        return jnp.where(ids < counts_row, all_prob * gap, 0.0)

    def combine(slot, h):
        at = lanes(slot, h)
        out = vs[slot, 0, :, piece(h)] * scales[0:1, at]
        for p in range(1, passages):
            out = out + vs[slot, p, :, piece(h)] * scales[p : p + 1, at]
        return out

    def g_forward(h):
        return remote(f_send.at[h], f_recv.at[h], g_ss.at[0, h], g_rs.at[0, h], sib)

    def g_direct(h):
        return remote(d_send.at[h], d_recv.at[h], g_ss.at[1, h], g_rs.at[1, h], peer(2 * core - 3))

    def g_two(h):
        return remote(t_send.at[h], t_recv.at[h], g_ss.at[2, h], g_rs.at[2, h], peer(-2))

    gaps = []
    for h in range(PARTS):
        gaps.append(score_part(h))
        f_send[h] = combine(FORWARD, h).astype(bf16)
        g_forward(h).start()
        d_send[h] = combine(DIRECT, h).astype(bf16)
        g_direct(h).start()
        two = combine(TWO, h)
        g_forward(h).wait_recv()
        t_send[h] = (two + f_recv[h].astype(f32)).astype(bf16)
        g_two(h).start()
    for h in range(PARTS):
        gown[:, piece(h)] = combine(OWN, h)
    gap = gaps[0]
    which = lax.broadcasted_iota(jnp.int32, (cand, LANES), 1) % queries // part_q
    for h in range(1, PARTS):
        gap = jnp.where(which == h, gaps[h], gap)
    loss = jnp.sum(gap, axis=0, keepdims=True)
    loss_ref[...] = loss[:, :queries]

    for p in range(passages):
        total_p = None
        for slot in range(CYCLE):
            for h in range(PARTS):
                at = lanes(slot, h)
                scaled = (qt[slot, h].astype(f32) * scales[p : p + 1, at]).astype(bf16)
                term = dot16(exps[p, :, at], scaled, NT)
                total_p = term if total_p is None else total_p + term
        pg[:, p, :] = total_p[:p_tokens]
    for c in range(6):
        at = slice(c * step, (c + 1) * step)
        tokens = slice(c * step // passages, (c + 1) * step // passages)
        v = pv[tokens].reshape(step, LANES)
        g = pg[tokens].reshape(step, LANES)
        raw_g = (g - v * jnp.sum(v * g, axis=1, keepdims=True)) * pinv[at]
        rg[at] = raw_g.astype(bf16)
    pterm[...] = dot16(rg[...], ph[...], TN)

    chunk = grad_ref.shape[0]
    width = qh.shape[1]

    def part_copy(k):
        return remote(part.at[peer(k)], part_recv.at[k], part_ss.at[k], part_rs.at[k], peer(k))

    for h in range(PARTS):
        g_direct(h).wait_recv()
        g_two(h).wait_recv()
        v = qv[:, piece(h)]
        g = gown[:, piece(h)] + d_recv[h].astype(f32) + t_recv[h].astype(f32)
        raw_g = (g - v * jnp.sum(v * g, axis=0, keepdims=True)) * qinv[:, piece(h)]
        raw_g = raw_g.astype(bf16)
        if h + 1 < PARTS:
            pterm[...] += dot16(raw_g, qh[piece(h)], NN)
    for c in range(2):
        cols = slice(c * width // 2, (c + 1) * width // 2)
        whole = jnp.transpose(pterm[:, cols] + dot16(raw_g, qh[piece(PARTS - 1), cols], NN))
        for k in range(n // 2):
            part[c * n // 2 + k] = whole[k * chunk : (k + 1) * chunk].astype(bf16)

        @pl.loop(c * n // 2, (c + 1) * n // 2)
        def _(i):
            t = i // 2 * 2 + lax.rem(i + me, 2)

            @pl.when(me != t)
            def _():
                part_copy(lax.rem(t - me + n, n)).start()

    grad_ref[...] = part[me].astype(f32)

    @pl.loop(1, n)
    def _(k):
        part_copy(k).wait_recv()
        grad_ref[...] += part_recv[k].astype(f32)

    for h in range(PARTS):
        q_two(h).wait_send()
        q_direct(h).wait_send()
        q_forward(h).wait_send()
        g_forward(h).wait_send()
        g_direct(h).wait_send()
        g_two(h).wait_send()
    for h in range(PARTS):
        for k in shifts:
            z_copy(k, h).wait_send()
    teach_across.wait_send()

    @pl.loop(1, n // 2)
    def _(k):
        teach_send(k).wait_send()

    @pl.loop(1, n)
    def _(k):
        part_copy(k).wait_send()


def per_device(
    n, query_hidden, passage_hidden, projection, teacher_rows, teacher_pos, neg_count, pass_len
):
    queries, q_tokens, width = query_hidden.shape
    passages, p_tokens, _ = passage_hidden.shape
    dim = projection.shape[1]
    q_rows = queries * q_tokens
    p_rows = passages * p_tokens
    padded = -(-p_tokens // 16) * 16
    chunk = width // n
    f32, bf16, i32 = jnp.float32, jnp.bfloat16, jnp.int32
    vmem = pl.BlockSpec(memory_space=pltpu.VMEM)
    hbm = pl.BlockSpec(memory_space=pltpu.HBM)
    dma = pltpu.SemaphoreType.DMA
    loss, grad_w = pl.pallas_call(
        functools.partial(kernel, n, queries, q_tokens, passages, p_tokens),
        out_shape=(
            jax.ShapeDtypeStruct((1, queries), f32),
            jax.ShapeDtypeStruct((chunk, dim), f32),
        ),
        in_specs=[hbm] * 7,
        out_specs=(vmem, vmem),
        scratch_shapes=[
            pltpu.VMEM((q_rows, width), bf16),
            pltpu.VMEM((p_rows, width), bf16),
            pltpu.VMEM((width, dim), bf16),
            pltpu.VMEM((queries, CYCLE * passages), f32),
            pltpu.VMEM((1, queries), i32),
            pltpu.VMEM((1, queries), i32),
            pltpu.SMEM((1, passages), i32),
            dma((6 + PARTS,)),
            pltpu.VMEM((2, n // 2, META, LANES), f32),
            pltpu.VMEM((dim, q_rows), f32),
            pltpu.VMEM((1, q_rows), f32),
            pltpu.VMEM((CYCLE, PARTS, dim, q_rows // PARTS), bf16),
            pltpu.VMEM((p_tokens, passages, dim), f32),
            pltpu.VMEM((p_rows, dim), f32),
            pltpu.VMEM((passages, padded, dim), bf16),
            pltpu.VMEM((passages, dim, padded), bf16),
            pltpu.VMEM((passages, padded, CYCLE * q_rows), bf16),
            pltpu.VMEM((passages, CYCLE * q_rows), f32),
            pltpu.VMEM((passages, CYCLE * q_rows), f32),
            pltpu.VMEM((CYCLE, passages, dim, q_rows), f32),
            pltpu.VMEM((CYCLE * q_rows, LANES), bf16),
            pltpu.VMEM((p_tokens, passages, dim), f32),
            pltpu.VMEM((p_rows, dim), bf16),
            pltpu.VMEM((dim, width), f32),
            pltpu.VMEM((dim, q_rows), f32),
            pltpu.VMEM((PARTS, passages, LANES), f32),
            pltpu.VMEM((PARTS, 2 * CYCLE - 1, passages, LANES), f32),
        ]
        + [pltpu.VMEM((PARTS, dim, q_rows // PARTS), bf16)] * 6
        + [
            pltpu.VMEM((n, chunk, dim), bf16),
            pltpu.VMEM((n, chunk, dim), bf16),
            dma((n // 2,)), dma((n // 2,)),
            dma((3, PARTS)), dma((3, PARTS)),
            dma((PARTS, 2 * CYCLE - 1)), dma((PARTS, 2 * CYCLE - 1)),
            dma((3, PARTS)), dma((3, PARTS)),
            dma((n,)), dma((n,)),
        ],
        compiler_params=pltpu.CompilerParams(
            collective_id=0, has_side_effects=True, vmem_limit_bytes=50 * 1024 * 1024
        ),
    )(
        *[
            pltpu.with_memory_space_constraint(x, pltpu.HBM)
            for x in (
                query_hidden.reshape(q_rows, width),
                jnp.transpose(passage_hidden, (1, 0, 2)).reshape(p_rows, width),
                projection,
                teacher_rows,
                teacher_pos.reshape(1, queries),
                neg_count.reshape(1, queries),
                pass_len.reshape(1, passages),
            )
        ]
    )
    def results(loss_in, grad_in, loss_out, grad_out, sem):
        first = pltpu.make_async_copy(loss_in, loss_out, sem.at[0])
        second = pltpu.make_async_copy(grad_in, grad_out, sem.at[1])
        first.start()
        second.start()
        first.wait()
        second.wait()

    loss, grad_w = pl.pallas_call(
        results,
        out_shape=(
            jax.ShapeDtypeStruct((1, queries), f32),
            jax.ShapeDtypeStruct((chunk, dim), f32),
        ),
        in_specs=[vmem, vmem],
        out_specs=(hbm, hbm),
        scratch_shapes=[dma((2,))],
        compiler_params=pltpu.CompilerParams(vmem_limit_bytes=1024 * 1024),
    )(loss, grad_w)
    return (loss.reshape(queries), grad_w)


def solution(mesh):
    return jax.shard_map(
        functools.partial(per_device, mesh.shape["blk"]),
        mesh=mesh,
        in_specs=(
            P(("groups", "blk"), None, None),
            P(("groups", "blk"), None, None),
            P(),
            P(("groups", "blk"), None),
            P(("groups", "blk")),
            P(("groups", "blk")),
            P(("groups", "blk")),
        ),
        out_specs=(P(("groups", "blk")), P(("groups", "blk"), None)),
        check_vma=False,
    )
```
